32 devices in a mesh: seq: 8 (over z, y), head: 4 (over x, core).
Axes of the slice: x: 2, y: 2, z: 4, core: 2. Of those that a mesh axis runs over, the one named last changes fastest.
Arguments:
- x_in: bfloat16 [1024, 8192], P('seq', 'head'), may hold values from -6 to 6
- bc_in: bfloat16 [1024, 2, 128], P('seq'), may hold values from -0.59765625 to 0.59765625
- conv_x: bfloat16 [4, 8192], P(None, 'head'), may hold values from -3 to 3
- conv_bc: bfloat16 [4, 2, 128], replicated, may hold values from -3 to 3
- log_decay: float32 [1024, 64], P('seq', 'head'), may hold values from -2 to 0, as said below
- skip: float32 [64], P('head'), may hold values from 0.5 to 1.5
- queries: bfloat16 [1024, 8192], P('seq', 'head'), may hold values from -12 to 12
- keys: bfloat16 [1024, 1024], P('seq', 'head'), may hold values from -5 to 5
- values: bfloat16 [1024, 1024], P('seq', 'head'), may hold values from -6 to 6
- d_mixed: bfloat16 [1024, 8192], P('seq', 'head'), may hold values from -6 to 6
Outputs:
- mixed: bfloat16 [1024, 8192], P('seq', 'head')
- d_queries: float32 [1024, 8192], P('seq', 'head')
- d_keys: float32 [1024, 1024], P('seq', 'head')
- d_values: float32 [1024, 1024], P('seq', 'head')
- d_x_in: float32 [1024, 8192], P('seq', 'head')
- d_bc_in: float32 [1024, 2, 128], P('seq')
- d_log_decay: float32 [1024, 64], P('seq', 'head')
The draws below stay inside these ranges and needn't reach their ends.
Inputs may be any that keep to these rules, and one draw needn't show every extreme that they name: `log_decay`: every entry is negative.
All inputs are finite; a program needn't handle non-finite values.
Results may differ from the reference program's by a relative error of at most 0.012.
The reference program's roundings to bfloat16 on the way count: a program that leaves them out, or rounds other values in their place, can miss the bound.
Values may be sent and summed in bfloat16 or wider, within the bound.
A program may use at most 128 MiB of HBM per device.

```python
import math
from functools import partial
import jax
import jax.numpy as jnp
from jax import lax

TOK_DEV = 128
SEQ = 1024
SSM_HEADS = 64
SSM_DIM = 128
STATE = 128
CONV = 4
Q_HEADS = 64
KV_HEADS = 8
HEAD_DIM = 128


def draw_log_decay(key, part):
    subkeys = jax.random.split(key, 7)
    share = 5
    fast = jax.random.randint(subkeys[0], (SSM_HEADS,), 0, 10) < share
    fast_rate = jax.random.uniform(subkeys[1], (SSM_HEADS,), jnp.float32, 0.02, 0.04)
    slow_rate = jax.random.uniform(subkeys[2], (SSM_HEADS,), jnp.float32, 0.1, 0.3) / SEQ
    descent_stepsize = jnp.where(fast, fast_rate, slow_rate)
    multiplier_coefficient = jnp.exp(jax.random.uniform(subkeys[3], (SEQ // TOK_DEV, 1, SSM_HEADS), jnp.float32, -0.7, 0.7))
    multiplier_coefficient = jnp.broadcast_to(multiplier_coefficient, (SEQ // TOK_DEV, TOK_DEV, SSM_HEADS)).reshape(SEQ, SSM_HEADS)
    approximate_guess = jnp.exp(jax.random.uniform(subkeys[4], (SEQ, SSM_HEADS), jnp.float32, -0.7, 0.7))
    sequence_slots = jax.random.randint(subkeys[5], (2, SSM_HEADS), 0, SEQ)
    number_of_branches = jax.random.uniform(subkeys[6], (2, SSM_HEADS), jnp.float32, 0.22, 0.7)
    element_indices = jnp.arange(SEQ, dtype=jnp.int32)[:, None, None]
    span_count = jnp.sum(jnp.where(element_indices == sequence_slots[None], number_of_branches[None], 0.0), axis=1)
    return -(descent_stepsize[None, :] * multiplier_coefficient * approximate_guess) - span_count


def draw_keys(key, part):
    base_key = jax.random.fold_in(key, 202)
    shape = (SEQ, KV_HEADS, HEAD_DIM)
    result = jnp.clip(jax.random.normal(base_key, shape, jnp.float32), -5.0, 5.0)
    return result.reshape(SEQ, KV_HEADS * HEAD_DIM).astype(jnp.bfloat16)


def draw_queries(key, part):
    base_key = jax.random.fold_in(key, 303)
    ratio = Q_HEADS // KV_HEADS
    shape = (SEQ, KV_HEADS, ratio, HEAD_DIM)
    result = jnp.clip(2.5 * jax.random.normal(base_key, shape, jnp.float32), -12.0, 12.0)
    return result.reshape(SEQ, Q_HEADS * HEAD_DIM).astype(jnp.bfloat16)


def block_levels(own_key, extent, pieces, least, largest):
    gain, own = 1.0, jax.random.fold_in(own_key, 6)
    for position, shards_of in pieces:
        draws = jnp.exp(jax.random.uniform(jax.random.fold_in(own, position), (shards_of,), jnp.float32, least / len(pieces), largest / len(pieces)))
        gain = gain * jnp.repeat(draws, extent[position] // shards_of).reshape([-1 if axis == position else 1 for axis in range(len(extent))])
    return gain


def gaussian(rng, shape, scale, most, shards=(), kind=jnp.bfloat16):
    loudness = block_levels(rng, shape, shards, -0.22, 0.18) if shards else 1.0
    entries = jax.random.normal(rng, shape, jnp.float32) * scale * loudness
    return jnp.minimum(jnp.maximum(entries, -most), most).astype(kind)


def setup_inputs(seed: int = 0) -> dict:
    key_of = jax.random.split(jax.random.key(seed), 11)
    x_in = gaussian(key_of[0], (SEQ, SSM_HEADS * SSM_DIM), 1.0, 6.0, ((0, 8), (1, 4)))
    bc_in = gaussian(key_of[1], (SEQ, 2, STATE), 0.1, 0.59765625, ((0, 8),))
    conv_x = gaussian(key_of[2], (CONV, SSM_HEADS * SSM_DIM), CONV ** -0.5, 3.0, ((1, 4),))
    conv_bc = gaussian(key_of[3], (CONV, 2, STATE), CONV ** -0.5, 3.0)
    log_decay = draw_log_decay(jax.random.fold_in(key_of[10], 71), 0)
    skip = jnp.clip(0.5 + 1.0 * jax.random.uniform(key_of[5], (SSM_HEADS,), jnp.float32) ** block_levels(key_of[5], (SSM_HEADS,), ((0, 4),), -0.2, 0.2), 0.5, 1.5)
    queries = draw_queries(jax.random.fold_in(key_of[10], 71), 0)
    keys = draw_keys(jax.random.fold_in(key_of[10], 71), 0)
    values = gaussian(key_of[8], (SEQ, KV_HEADS * HEAD_DIM), 1.0, 6.0, ((0, 8), (1, 4)))
    d_mixed = gaussian(key_of[9], (SEQ, SSM_HEADS * SSM_DIM), 1.0, 6.0, ((0, 8), (1, 4)))
    return {"x_in": x_in, "bc_in": bc_in, "conv_x": conv_x, "conv_bc": conv_bc, "log_decay": log_decay, "skip": skip, "queries": queries, "keys": keys, "values": values, "d_mixed": d_mixed}


masked_value = -1e+30
highest_precision = lax.Precision.HIGHEST

def silu_slope(pre):
    sigmoid = jax.nn.sigmoid(pre)
    return sigmoid * (1.0 + pre * (1.0 - sigmoid))

def conv_forward(inputs, before, weight):
    padded = jnp.concatenate([before, inputs], axis=0)
    length = inputs.shape[0]
    total = jnp.zeros(inputs.shape, jnp.float32)
    for tap in range(weight.shape[0]):
        total = total + weight[tap].astype(jnp.float32) * padded[tap:tap + length].astype(jnp.float32)
    return total

def conv_backward(grads, after, weight):
    width = weight.shape[0]
    padded = jnp.concatenate([grads, after], axis=0)
    length = grads.shape[0]
    total = jnp.zeros(grads.shape, jnp.float32)
    for tap in range(width):
        offset = width - 1 - tap
        total = total + weight[tap].astype(jnp.float32) * padded[offset:offset + length]
    return total

def span_step(state, x_blk, b_blk, c_blk, a_blk, skip):
    size = x_blk.shape[0]
    running = jnp.cumsum(a_blk, axis=0)
    gaps = running[:, None, :] - running[None, :, :]
    order = jnp.arange(size, dtype=jnp.int32)
    allowed = (order[:, None] >= order[None, :])[:, :, None]
    fading = jnp.exp(jnp.where(allowed, gaps, masked_value))
    inner = jnp.dot(c_blk, b_blk.T, precision=highest_precision)
    outputs = jnp.einsum('tsh,shp->thp', inner[:, :, None] * fading, x_blk, precision=highest_precision)
    carried = jnp.einsum('tn,hpn->thp', c_blk, state, precision=highest_precision)
    outputs = outputs + jnp.exp(running)[:, :, None] * carried + skip[None, :, None] * x_blk
    final = running[-1]
    tail_fade = jnp.exp(final[None, :] - running)
    state = jnp.exp(final)[:, None, None] * state + jnp.einsum('sh,shp,sn->hpn', tail_fade, x_blk, b_blk, precision=highest_precision)
    return (outputs, state)

def ssd_run(x_rows, b_rows, c_rows, decay, skip):
    size = math.gcd(128, TOK_DEV)
    blocks = SEQ // size
    x_blocks = x_rows.reshape(blocks, size, SSM_HEADS, SSM_DIM)
    b_blocks = b_rows.reshape(blocks, size, STATE)
    c_blocks = c_rows.reshape(blocks, size, STATE)
    a_blocks = decay.reshape(blocks, size, SSM_HEADS)

    def advance(state, item):
        x_blk, b_blk, c_blk, a_blk = item
        outputs, state = span_step(state, x_blk, b_blk, c_blk, a_blk, skip)
        return (state, outputs)
    initial = jnp.zeros((SSM_HEADS, SSM_DIM, STATE), x_rows.dtype)
    _, outputs = lax.scan(advance, initial, (x_blocks, b_blocks, c_blocks, a_blocks))
    return outputs.reshape(SEQ, SSM_HEADS, SSM_DIM)

def reference(x_in, bc_in, conv_x, conv_bc, log_decay, skip, queries, keys, values, d_mixed):
    edge = CONV - 1
    pre_x = conv_forward(x_in, jnp.zeros((edge, x_in.shape[1]), x_in.dtype), conv_x)
    pre_bc = conv_forward(bc_in, jnp.zeros((edge,) + bc_in.shape[1:], bc_in.dtype), conv_bc)
    x_conv = jax.nn.silu(pre_x).astype(jnp.bfloat16)
    bc_conv = jax.nn.silu(pre_bc).astype(jnp.bfloat16)
    x_rows = x_conv.astype(jnp.float32).reshape(SEQ, SSM_HEADS, SSM_DIM)
    b_rows = bc_conv[:, 0].astype(jnp.float32)
    c_rows = bc_conv[:, 1].astype(jnp.float32)
    ssm_out, ssd_back = jax.vjp(partial(ssd_run, skip=skip), x_rows, b_rows, c_rows, log_decay)
    ratio = Q_HEADS // KV_HEADS
    softmax_scale = HEAD_DIM ** (-0.5)
    query_heads = queries.reshape(SEQ, Q_HEADS, HEAD_DIM).transpose(1, 0, 2)
    grad_heads = d_mixed.reshape(SEQ, Q_HEADS, HEAD_DIM).transpose(1, 0, 2)
    key_heads = keys.reshape(SEQ, KV_HEADS, HEAD_DIM).transpose(1, 0, 2)
    value_heads = values.reshape(SEQ, KV_HEADS, HEAD_DIM).transpose(1, 0, 2)
    order = jnp.arange(SEQ, dtype=jnp.int32)
    allowed = order[None, :] <= order[:, None]

    def one_head(head):
        group = head // ratio
        query = query_heads[head]
        grad = grad_heads[head]
        key_rows = key_heads[group]
        value_rows = value_heads[group]
        attention_scores = jnp.where(allowed, jnp.dot(query, key_rows.T, preferred_element_type=jnp.float32) * softmax_scale, masked_value)
        top = lax.optimization_barrier(jnp.max(attention_scores, axis=-1))
        lse = top + jnp.log(lax.optimization_barrier(jnp.sum(jnp.exp(attention_scores - top[:, None]), axis=-1)))
        probs = jnp.exp(attention_scores - lse[:, None])
        attention_weights = probs.astype(jnp.bfloat16)
        attended_output = jnp.dot(attention_weights, value_rows, preferred_element_type=jnp.float32)
        delta_terms = lax.optimization_barrier(jnp.sum(grad.astype(jnp.float32) * attended_output, axis=-1))
        weight_gradient = jnp.dot(grad, value_rows.T, preferred_element_type=jnp.float32)
        score_gradient = (probs * (weight_gradient - delta_terms[:, None])).astype(jnp.bfloat16)
        dquery = jnp.dot(score_gradient, key_rows, preferred_element_type=jnp.float32) * softmax_scale
        dkey = jnp.dot(score_gradient.T, query, preferred_element_type=jnp.float32) * softmax_scale
        value_gradient = jnp.dot(attention_weights.T, grad, preferred_element_type=jnp.float32)
        return (attended_output, dquery, dkey, value_gradient)
    attended_output, dquery, dkey, value_gradient = lax.map(one_head, jnp.arange(Q_HEADS, dtype=jnp.int32))
    attended_flat = attended_output.transpose(1, 0, 2).reshape(SEQ, Q_HEADS * HEAD_DIM)
    mixed = (ssm_out.reshape(SEQ, SSM_HEADS * SSM_DIM) + attended_flat).astype(jnp.bfloat16)
    d_queries = dquery.transpose(1, 0, 2).reshape(SEQ, Q_HEADS * HEAD_DIM)
    d_keys = dkey.reshape(KV_HEADS, ratio, SEQ, HEAD_DIM).sum(axis=1).transpose(1, 0, 2).reshape(SEQ, KV_HEADS * HEAD_DIM)
    d_values = value_gradient.reshape(KV_HEADS, ratio, SEQ, HEAD_DIM).sum(axis=1).transpose(1, 0, 2).reshape(SEQ, KV_HEADS * HEAD_DIM)
    grad_y = d_mixed.astype(jnp.float32).reshape(SEQ, SSM_HEADS, SSM_DIM)
    grad_x, grad_b, grad_c, d_log_decay = ssd_back(grad_y)
    grad_pre_x = grad_x.reshape(SEQ, SSM_HEADS * SSM_DIM) * silu_slope(pre_x)
    grad_pre_bc = jnp.stack([grad_b, grad_c], axis=1) * silu_slope(pre_bc)
    d_x_in = conv_backward(grad_pre_x, jnp.zeros((edge, grad_pre_x.shape[1]), jnp.float32), conv_x)
    d_bc_in = conv_backward(grad_pre_bc, jnp.zeros((edge,) + grad_pre_bc.shape[1:], jnp.float32), conv_bc)
    return (mixed, d_queries, d_keys, d_values, d_x_in, d_bc_in, d_log_decay)
```

```python
import functools
import math

import jax
import jax.numpy as jnp
from jax import lax
from jax.experimental import pallas as pl
from jax.experimental.pallas import tpu as pltpu
from jax.sharding import PartitionSpec as P

D = 128
EDGE = 16
F32 = jnp.float32
BF16 = jnp.bfloat16
MESH = pl.DeviceIdType.MESH
VMEM = pl.BlockSpec(memory_space=pltpu.VMEM)
ANY = pl.BlockSpec(memory_space=pl.ANY)


def mm(a, b):
    return jnp.dot(a, b, preferred_element_type=F32)


def mm_nt(a, b):
    return lax.dot_general(a, b, (((1,), (1,)), ((), ())), preferred_element_type=F32)


def sigmoid(v):
    return 1.0 / (1.0 + jnp.exp(-v))


def peer(**coords):
    return dict(device_id=coords, device_id_type=MESH)


def gather_kernel(n, x_ref, bc_ref, k_ref, v_ref, xh, bch, bcn, ka, va,
                  ks, kr, vs, vr, hs, hr, loc):
    me = lax.axis_index("seq")
    rows = x_ref.shape[0]
    barrier = pltpu.get_barrier_semaphore()
    for off in range(1, n):
        pl.semaphore_signal(barrier, inc=1, **peer(seq=lax.rem(me + off, n)))
    pl.semaphore_wait(barrier, n - 1)

    def halo(slot, src, dst, to):
        return pltpu.make_async_remote_copy(
            src_ref=src, dst_ref=dst, send_sem=hs.at[slot], recv_sem=hr.at[slot], **peer(seq=to))

    nxt = lax.rem(me + 1, n)
    prv = lax.rem(me + n - 1, n)
    last = pl.ds(rows - EDGE, EDGE)
    cx = halo(0, x_ref.at[last], xh, nxt)
    cb = halo(1, bc_ref.at[last], bch, nxt)
    cn = halo(2, bc_ref.at[pl.ds(0, EDGE)], bcn, prv)

    @pl.when(me < n - 1)
    def _():
        cx.start()
        cb.start()

    @pl.when(me > 0)
    def _():
        cn.start()

    lk = pltpu.make_async_copy(k_ref, ka.at[me], loc.at[0])
    lv = pltpu.make_async_copy(v_ref, va.at[me], loc.at[1])
    lk.start()
    lv.start()

    def pair(off, to):
        return (
            pltpu.make_async_remote_copy(
                src_ref=k_ref, dst_ref=ka.at[me], send_sem=ks.at[off], recv_sem=kr.at[off],
                **peer(seq=to)),
            pltpu.make_async_remote_copy(
                src_ref=v_ref, dst_ref=va.at[me], send_sem=vs.at[off], recv_sem=vr.at[off],
                **peer(seq=to)),
        )

    for off in range(1, n):
        @pl.when(me + off < n)
        def _():
            a, b = pair(off, lax.rem(me + off, n))
            a.start()
            b.start()

    for off in range(1, n):
        @pl.when(me + off < n)
        def _():
            slot = lax.rem(me + off, n)
            ka[slot] = jnp.zeros(ka.shape[1:], ka.dtype)
            va[slot] = jnp.zeros(va.shape[1:], va.dtype)

    @pl.when(me == 0)
    def _():
        xh[...] = jnp.zeros(xh.shape, xh.dtype)
        bch[...] = jnp.zeros(bch.shape, bch.dtype)

    @pl.when(me == n - 1)
    def _():
        bcn[...] = jnp.zeros(bcn.shape, bcn.dtype)

    @pl.when(me < n - 1)
    def _():
        cx.wait_send()
        cb.wait_send()
        cn.wait_recv()

    @pl.when(me > 0)
    def _():
        cn.wait_send()
        cx.wait_recv()
        cb.wait_recv()

    lk.wait()
    lv.wait()
    for off in range(1, n):
        @pl.when(me + off < n)
        def _():
            a, b = pair(off, lax.rem(me + off, n))
            a.wait_send()
            b.wait_send()

        @pl.when(me - off >= 0)
        def _():
            a, b = pair(off, prv)
            a.wait_recv()
            b.wait_recv()


def gather(n, x_in, bc, keys, values):
    rows, width = keys.shape
    dma = pltpu.SemaphoreType.DMA
    return pl.pallas_call(
        functools.partial(gather_kernel, n),
        out_shape=(
            jax.ShapeDtypeStruct((EDGE, x_in.shape[1]), BF16),
            jax.ShapeDtypeStruct((EDGE, bc.shape[1]), BF16),
            jax.ShapeDtypeStruct((EDGE, bc.shape[1]), BF16),
            jax.ShapeDtypeStruct((n, rows, width), BF16),
            jax.ShapeDtypeStruct((n, rows, width), BF16),
        ),
        in_specs=[ANY] * 4,
        out_specs=(VMEM,) * 5,
        scratch_shapes=[dma((n,)), dma((n,)), dma((n,)), dma((n,)), dma((3,)), dma((3,)), dma((2,))],
        compiler_params=pltpu.CompilerParams(
            collective_id=0, has_side_effects=True, vmem_limit_bytes=40 * 2**20),
        name="gather",
    )(x_in, bc, keys, values)


def conv(x, halo, taps):
    width = taps.shape[0]
    rows = x.shape[0]
    full = jnp.concatenate([halo[EDGE - 8:], x], axis=0)
    total = None
    for tap in range(width):
        start = 8 - (width - 1) + tap
        term = taps[tap:tap + 1] * full[start:start + rows]
        total = term if total is None else total + term
    return total


def columns(row):
    return jnp.transpose(jnp.broadcast_to(row, (D, row.shape[1])))


def own_kernel(x_ref, xh_ref, w_ref, bc_ref, bch_ref, wbc_ref, run_ref, dm_ref,
               bcv_ref, of_ref, ob_ref, bt, ct):
    @pl.when(pl.program_id(0) == 0)
    def _():
        pre = conv(bc_ref[...].astype(F32), bch_ref[...].astype(F32), wbc_ref[...].astype(F32))
        act = pre * sigmoid(pre)
        bcv_ref[...] = act.astype(BF16)
        act = act.astype(BF16).astype(F32)
        bt[...] = jnp.transpose(act[:, :D]).astype(BF16)
        ct[...] = jnp.transpose(act[:, D:]).astype(BF16)

    pre = conv(x_ref[...].astype(F32), xh_ref[...].astype(F32), w_ref[...].astype(F32))
    xc = (pre * sigmoid(pre)).astype(BF16).astype(F32)
    row = run_ref[0]
    col = columns(row)
    final = row[:, row.shape[1] - 1:]
    of_ref[0] = mm(bt[...], (xc * jnp.exp(final - col)).astype(BF16))
    ob_ref[0] = mm(ct[...], (dm_ref[...].astype(F32) * jnp.exp(col)).astype(BF16))


def own_states(x_in, xh, conv_x, bc, bch, conv_bc, run_rows, d_mixed):
    rows, wide = x_in.shape
    heads = wide // D
    by_head = lambda r: pl.BlockSpec((r, D), lambda h: (0, h))
    whole = lambda a: pl.BlockSpec(a.shape, lambda h: (0,) * a.ndim)
    cube = pl.BlockSpec((1, D, D), lambda h: (h, 0, 0))
    return pl.pallas_call(
        own_kernel,
        grid=(heads,),
        out_shape=(
            jax.ShapeDtypeStruct(bc.shape, BF16),
            jax.ShapeDtypeStruct((heads, D, D), F32),
            jax.ShapeDtypeStruct((heads, D, D), F32),
        ),
        in_specs=[by_head(rows), by_head(EDGE), by_head(conv_x.shape[0]), whole(bc), whole(bch),
                  whole(conv_bc), pl.BlockSpec((1, 1, rows), lambda h: (h, 0, 0)), by_head(rows)],
        out_specs=(whole(bc), cube, cube),
        scratch_shapes=[pltpu.VMEM((D, rows), BF16), pltpu.VMEM((D, rows), BF16)],
        name="own_states",
    )(x_in, xh, conv_x, bc, bch, conv_bc, run_rows, d_mixed)


def chain_kernel(n, size, of, ob, dec, s_in, g_in, sf, sb, fs, fr, bs, br):
    me = lax.axis_index("seq")
    chunks = of.shape[0] // size
    nxt = lax.rem(me + 1, n)
    prv = lax.rem(me + n - 1, n)
    barrier = pltpu.get_barrier_semaphore()
    for to in (nxt, prv):
        pl.semaphore_signal(barrier, inc=1, **peer(seq=to))
    pl.semaphore_wait(barrier, 2)

    def copy(stage, landing, send, recv, c, to):
        part = pl.ds(c * size, size)
        return pltpu.make_async_remote_copy(
            src_ref=stage.at[part], dst_ref=landing.at[part], send_sem=send.at[c],
            recv_sem=recv.at[c], **peer(seq=to))

    def hop(c, own, landing, stage, send, recv, to, first, last):
        part = pl.ds(c * size, size)

        @pl.when(first)
        def _():
            landing[part] = jnp.zeros((size,) + landing.shape[1:], landing.dtype)
            stage[part] = own[part].astype(BF16)

        @pl.when(jnp.logical_not(first))
        def _():
            copy(stage, landing, send, recv, c, to).wait_recv()

            @pl.when(jnp.logical_not(last))
            def _():
                stage[part] = (dec[part] * landing[part].astype(F32) + own[part]).astype(BF16)

        @pl.when(jnp.logical_not(last))
        def _():
            copy(stage, landing, send, recv, c, to).start()

    def step(t, carry):
        f = t - me
        b = t - (n - 1 - me)

        @pl.when(jnp.logical_and(f >= 0, f < chunks))
        def _():
            hop(f, of, s_in, sf, fs, fr, nxt, me == 0, me == n - 1)

        @pl.when(jnp.logical_and(b >= 0, b < chunks))
        def _():
            hop(b, ob, g_in, sb, bs, br, prv, me == n - 1, me == 0)

        return carry

    lax.fori_loop(0, n - 1 + chunks, step, 0)

    def drain(c, carry):
        @pl.when(me < n - 1)
        def _():
            copy(sf, s_in, fs, fr, c, nxt).wait_send()

        @pl.when(me > 0)
        def _():
            copy(sb, g_in, bs, br, c, prv).wait_send()

        return carry

    lax.fori_loop(0, chunks, drain, 0)


def chain(n, of, ob, dec):
    heads = of.shape[0]
    size = 2 if heads % 2 == 0 else 1
    chunks = heads // size
    dma = pltpu.SemaphoreType.DMA
    out = jax.ShapeDtypeStruct(of.shape, BF16)
    return pl.pallas_call(
        functools.partial(chain_kernel, n, size),
        out_shape=(out, out),
        in_specs=[VMEM] * 3,
        out_specs=(VMEM, VMEM),
        scratch_shapes=[pltpu.VMEM(of.shape, BF16), pltpu.VMEM(of.shape, BF16),
                        dma((chunks,)), dma((chunks,)), dma((chunks,)), dma((chunks,))],
        compiler_params=pltpu.CompilerParams(
            collective_id=1, has_side_effects=True, vmem_limit_bytes=40 * 2**20),
        name="chain",
    )(of, ob, dec)


def main_kernel(ratio, heads, pos_ref, x_ref, xh_ref, w_ref, dm_ref, q_ref, bcv_ref, run_ref,
                skip_ref, k_ref, v_ref, s_ref, g_ref,
                mixed_ref, dq_ref, dk_ref, dv_ref, dx_ref, gh_ref, dla_ref, dbc_ref,
                kt, vt, inner, dinner, dka, dva, dbc):
    h = pl.program_id(0)
    rows = x_ref.shape[0]
    scale = D ** (-0.5)
    b = bcv_ref[:, :D]
    c = bcv_ref[:, D:]

    @pl.when(h == 0)
    def _():
        inner[...] = mm_nt(c, b)
        dinner[...] = jnp.zeros_like(dinner)
        dbc[...] = jnp.zeros_like(dbc)

    @pl.when(lax.rem(h, ratio) == 0)
    def _():
        kt[...] = jnp.transpose(k_ref[...].astype(F32)).astype(BF16)
        vt[...] = jnp.transpose(v_ref[...].astype(F32)).astype(BF16)
        dka[...] = jnp.zeros_like(dka)
        dva[...] = jnp.zeros_like(dva)

    dm = dm_ref[...]
    dmf = dm.astype(F32)
    q = q_ref[...]
    s = mm_nt(k_ref[...], q)
    upos = lax.broadcasted_iota(jnp.int32, s.shape, 0)
    tpos = lax.broadcasted_iota(jnp.int32, s.shape, 1) + pos_ref[0]
    s = jnp.where(upos <= tpos, s * (scale * math.log2(math.e)), -1e30)
    e = jnp.exp2(s - jnp.max(s, axis=0, keepdims=True))
    p = e * (1.0 / jnp.sum(e, axis=0, keepdims=True))
    pb = p.astype(BF16)
    att_t = mm(vt[...], pb)
    delta = jnp.sum(jnp.transpose(dmf) * att_t, axis=0, keepdims=True)
    ds = (p * (mm_nt(v_ref[...], dm) - delta)).astype(BF16)
    dq_ref[...] = jnp.transpose(mm(kt[...], ds)) * scale
    dka[...] += mm(ds, q)
    dva[...] += mm(pb, dm)

    @pl.when(lax.rem(h, ratio) == ratio - 1)
    def _():
        dk_ref[...] = (dka[...] * scale).astype(BF16)
        dv_ref[...] = dva[...].astype(BF16)

    w = w_ref[...].astype(F32)
    pre = conv(x_ref[...].astype(F32), xh_ref[...].astype(F32), w)
    sig = sigmoid(pre)
    xb = (pre * sig).astype(BF16)
    xf = xb.astype(F32)
    row = run_ref[0]
    col = columns(row)
    final = row[:, rows - 1:]
    t_i = lax.broadcasted_iota(jnp.int32, (rows, rows), 0)
    s_i = lax.broadcasted_iota(jnp.int32, (rows, rows), 1)
    fade = jnp.exp(jnp.where(t_i >= s_i, col - row, -1e30))
    mix = inner[...] * fade
    skip = skip_ref[0]
    enter = jnp.exp(col)
    tail = jnp.exp(final - col)
    state = s_ref[0]
    grad = g_ref[0]
    carried = enter * mm(c, state)
    y = mm(mix.astype(BF16), xb) + carried + skip * xf
    mixed_ref[...] = (y + jnp.transpose(att_t)).astype(BF16)
    back = tail * mm(b, grad)
    gx = mm(jnp.transpose(mix).astype(BF16), dm) + back + skip * dmf
    dmix = mm_nt(dm, xb)
    dinner[...] += dmix * fade
    dbc[:, D:] += mm_nt((enter * dmf).astype(BF16), state)
    dbc[:, :D] += mm_nt((tail * xf).astype(BF16), grad)
    dgap = dmix * mix
    away = xf * back
    net = dgap - jnp.transpose(dgap) + dmf * carried - away
    net = jnp.sum(net, axis=1, keepdims=True)
    dfinal = jnp.sum(away) + jnp.sum(
        jnp.exp(final) * jnp.sum(state.astype(F32) * grad.astype(F32), axis=0, keepdims=True))
    dla_ref[0] = jnp.sum(jnp.where(t_i >= s_i, net, 0.0), axis=0, keepdims=True) + dfinal

    g = gx * (sig * (1.0 + pre * (1.0 - sig)))
    gh_ref[...] = g[:EDGE].astype(BF16)
    width = w.shape[0]
    padded = jnp.concatenate([g, jnp.zeros((8, D), F32)], axis=0)
    total = None
    for tap in range(width):
        offset = width - 1 - tap
        term = w[tap:tap + 1] * padded[offset:offset + rows]
        total = term if total is None else total + term
    dx_ref[...] = total

    @pl.when(h == heads - 1)
    def _():
        di = dinner[...]
        dbc_ref[:, D:] = (dbc[:, D:] + mm(di.astype(BF16), b)).astype(BF16)
        dbc_ref[:, :D] = (dbc[:, :D] + mm(jnp.transpose(di).astype(BF16), c)).astype(BF16)


def main_part(pos, x_in, xh, conv_x, d_mixed, queries, bcv, run_rows, skip_rows, ka, va, s_in, g_in):
    rows, wide = x_in.shape
    heads = wide // D
    length, kv_wide = ka.shape
    ratio = heads // (kv_wide // D)
    by_head = lambda r: pl.BlockSpec((r, D), lambda h: (0, h))
    whole = lambda a: pl.BlockSpec(a.shape, lambda h: (0,) * a.ndim)
    cube = pl.BlockSpec((1, D, D), lambda h: (h, 0, 0))
    line = lambda r: pl.BlockSpec((1, 1, r), lambda h: (h, 0, 0))
    by_kv = pl.BlockSpec((length, D), lambda h: (0, h // ratio))
    shape = jax.ShapeDtypeStruct
    return pl.pallas_call(
        functools.partial(main_kernel, ratio, heads),
        grid=(heads,),
        out_shape=(
            shape((rows, wide), BF16), shape((rows, wide), F32), shape((length, kv_wide), BF16),
            shape((length, kv_wide), BF16), shape((rows, wide), F32), shape((EDGE, wide), BF16),
            shape((heads, 1, rows), F32), shape(bcv.shape, BF16),
        ),
        in_specs=[pl.BlockSpec(memory_space=pltpu.SMEM), by_head(rows), by_head(EDGE),
                  by_head(conv_x.shape[0]), by_head(rows), by_head(rows), whole(bcv), line(rows),
                  line(D), by_kv, by_kv, cube, cube],
        out_specs=(by_head(rows), by_head(rows), by_kv, by_kv, by_head(rows), by_head(EDGE),
                   line(rows), whole(bcv)),
        scratch_shapes=[
            pltpu.VMEM((D, length), BF16), pltpu.VMEM((D, length), BF16),
            pltpu.VMEM((rows, rows), F32), pltpu.VMEM((rows, rows), F32),
            pltpu.VMEM((length, D), F32), pltpu.VMEM((length, D), F32),
            pltpu.VMEM(bcv.shape, F32),
        ],
        compiler_params=pltpu.CompilerParams(vmem_limit_bytes=48 * 2**20),
        name="heads",
    )(pos, x_in, xh, conv_x, d_mixed, queries, bcv, run_rows, skip_rows, ka, va, s_in, g_in)


def sums_kernel(n, m, dk_ref, dv_ref, bc_ref, gh_ref, dk_out, dv_out, bc_out, bcn_out, gn_out,
                kb, vb, bb, nb, ks, kr, vs, vr, bs, br, ns, nr, hs, hr):
    me = lax.axis_index("seq")
    my = lax.axis_index("head")
    nxt = lax.rem(me + 1, n)
    prv = lax.rem(me + n - 1, n)
    barrier = pltpu.get_barrier_semaphore()
    count = 0
    for off in range(1, n):
        pl.semaphore_signal(barrier, inc=1, **peer(seq=lax.rem(me + off, n), head=my))
        count += 1
    for off in range(1, m):
        other = lax.rem(my + off, m)
        for to in (me, nxt, prv):
            pl.semaphore_signal(barrier, inc=1, **peer(seq=to, head=other))
            count += 1
    pl.semaphore_wait(barrier, count)

    def remote(src, dst, send, recv, seq, head):
        return pltpu.make_async_remote_copy(
            src_ref=src, dst_ref=dst, send_sem=send, recv_sem=recv, **peer(seq=seq, head=head))

    def pair(off, to):
        to = lax.rem(to + n, n)
        return (remote(dk_ref.at[to], kb.at[off], ks.at[off], kr.at[off], to, my),
                remote(dv_ref.at[to], vb.at[off], vs.at[off], vr.at[off], to, my))

    def across(off):
        return remote(bc_ref, bb.at[off], bs.at[off], br.at[off], me, lax.rem(my + off, m))

    def before(off):
        return remote(bc_ref.at[pl.ds(0, EDGE)], nb.at[off], ns.at[off], nr.at[off], prv,
                      lax.rem(my + off, m))

    edge = remote(gh_ref, gn_out, hs, hr, prv, my)
    for off in range(1, n):
        @pl.when(me - off >= 0)
        def _():
            for cp in pair(off, me - off):
                cp.start()

    for off in range(1, m):
        across(off).start()

    @pl.when(me > 0)
    def _():
        edge.start()
        for off in range(m):
            before(off).start()

    total = bc_ref[...].astype(F32)
    for off in range(1, m):
        across(off).wait_recv()
        total += bb[off].astype(F32)
    bc_out[...] = total

    @pl.when(me < n - 1)
    def _():
        edge.wait_recv()
        after = None
        for off in range(m):
            before(off).wait_recv()
            part = nb[off].astype(F32)
            after = part if after is None else after + part
        bcn_out[...] = after

    @pl.when(me == n - 1)
    def _():
        gn_out[...] = jnp.zeros(gn_out.shape, gn_out.dtype)
        bcn_out[...] = jnp.zeros(bcn_out.shape, bcn_out.dtype)

    dk_out[...] = dk_ref[me].astype(F32)
    dv_out[...] = dv_ref[me].astype(F32)
    for off in range(1, n):
        @pl.when(me + off < n)
        def _():
            a, b = pair(off, me + off)
            a.wait_recv()
            b.wait_recv()
            dk_out[...] += kb[off].astype(F32)
            dv_out[...] += vb[off].astype(F32)

    for off in range(1, n):
        @pl.when(me - off >= 0)
        def _():
            for cp in pair(off, me - off):
                cp.wait_send()
    for off in range(1, m):
        across(off).wait_send()

    @pl.when(me > 0)
    def _():
        edge.wait_send()
        for off in range(m):
            before(off).wait_send()


def sums(n, m, dk, dv, dbc, gh):
    rows, width = dk.shape[1:]
    dma = pltpu.SemaphoreType.DMA
    shape = jax.ShapeDtypeStruct
    return pl.pallas_call(
        functools.partial(sums_kernel, n, m),
        out_shape=(shape((rows, width), F32), shape((rows, width), F32), shape(dbc.shape, F32),
                   shape((EDGE, dbc.shape[1]), F32), shape(gh.shape, BF16)),
        in_specs=[VMEM] * 4,
        out_specs=(VMEM,) * 5,
        scratch_shapes=[
            pltpu.VMEM((n, rows, width), BF16), pltpu.VMEM((n, rows, width), BF16),
            pltpu.VMEM((m,) + dbc.shape, BF16), pltpu.VMEM((m, EDGE, dbc.shape[1]), BF16),
            dma((n,)), dma((n,)), dma((n,)), dma((n,)), dma((m,)), dma((m,)), dma((m,)), dma((m,)),
            dma, dma],
        compiler_params=pltpu.CompilerParams(
            collective_id=2, has_side_effects=True, vmem_limit_bytes=40 * 2**20),
        name="sums",
    )(dk, dv, dbc, gh)


def silu_slope(pre):
    s = jax.nn.sigmoid(pre)
    return s * (1.0 + pre * (1.0 - s))


def shards(n, m, x_in, bc_in, conv_x, conv_bc, log_decay, skip, queries, keys, values, d_mixed):
    rows = x_in.shape[0]
    heads = x_in.shape[1] // D
    taps = conv_x.shape[0]
    edge = taps - 1
    bc = bc_in.reshape(rows, 2 * D)
    wbc = conv_bc.reshape(taps, 2 * D)
    xh, bch, bcn, ka, va = gather(n, x_in, bc, keys, values)
    running = jnp.cumsum(log_decay, axis=0)
    run_rows = running.T.reshape(heads, 1, rows)
    dec = jnp.broadcast_to(jnp.exp(running[-1])[:, None, None], (heads, 1, D))
    skip_rows = jnp.broadcast_to(skip[:, None, None], (heads, 1, D))
    bcv, of, ob = own_states(x_in, xh, conv_x, bc, bch, wbc, run_rows, d_mixed)
    s_in, g_in = chain(n, of, ob, dec)
    pos = (lax.axis_index("seq") * rows).astype(jnp.int32).reshape(1)
    mixed, dq, dk, dv, dx, gh, dla, dbc = main_part(
        pos, x_in, xh, conv_x, d_mixed, queries, bcv, run_rows, skip_rows,
        ka.reshape(n * rows, -1), va.reshape(n * rows, -1), s_in, g_in)
    d_keys, d_values, bcs, bca, gn = sums(
        n, m, dk.reshape(n, rows, -1), dv.reshape(n, rows, -1), dbc, gh)
    wx = conv_x.astype(F32)
    gnf = jnp.concatenate([jnp.zeros((edge, gn.shape[1]), F32), gn[:edge].astype(F32)], axis=0)
    fix = sum(wx[j] * gnf[edge - j:2 * edge - j] for j in range(taps))
    d_x_in = dx.at[rows - edge:].add(fix)
    wb = wbc.astype(F32)
    full = jnp.concatenate([bch[EDGE - edge:], bc, bcn[:edge]], axis=0).astype(F32)
    pre = sum(wb[j] * full[j:j + rows + edge] for j in range(taps))
    g = jnp.concatenate([bcs, bca[:edge]], axis=0) * silu_slope(pre)
    d_bc = sum(wb[j] * g[edge - j:edge - j + rows] for j in range(taps))
    return (mixed, dq, d_keys, d_values, d_x_in, d_bc.reshape(rows, 2, D), dla.reshape(heads, rows).T)


def solution(mesh):
    n, m = mesh.shape["seq"], mesh.shape["head"]
    grid = P("seq", "head")
    part = P("seq", None, None)
    in_specs = (grid, part, P(None, "head"), P(), grid, P("head"), grid, grid, grid, grid)
    out_specs = (grid, grid, grid, grid, grid, part, grid)
    return jax.shard_map(functools.partial(shards, n, m), mesh=mesh, in_specs=in_specs,
                         out_specs=out_specs, check_vma=False)
```

```python
import functools
import math

import jax
import jax.numpy as jnp
from jax import lax
from jax.experimental import pallas as pl
from jax.experimental.pallas import tpu as pltpu
from jax.sharding import PartitionSpec as P

D = 128
EDGE = 16
F32 = jnp.float32
BF16 = jnp.bfloat16
MESH = pl.DeviceIdType.MESH
VMEM = pl.BlockSpec(memory_space=pltpu.VMEM)
ANY = pl.BlockSpec(memory_space=pl.ANY)


def mm(a, b):
    return jnp.dot(a, b, preferred_element_type=F32)


def mm_nt(a, b):
    return lax.dot_general(a, b, (((1,), (1,)), ((), ())), preferred_element_type=F32)


def sigmoid(v):
    return 1.0 / (1.0 + jnp.exp(-v))


def peer(**coords):
    return dict(device_id=coords, device_id_type=MESH)


def conv(x, halo, taps):
    width = taps.shape[0]
    rows = x.shape[0]
    full = jnp.concatenate([halo[EDGE - 8:], x], axis=0)
    total = None
    for tap in range(width):
        start = 8 - (width - 1) + tap
        term = taps[tap:tap + 1] * full[start:start + rows]
        total = term if total is None else total + term
    return total


def columns(row):
    return jnp.transpose(jnp.broadcast_to(row, (D, row.shape[1])))


def first_kernel(n, x_ref, bc_ref, k_ref, v_ref, w_ref, wbc_ref, run_ref, dm_ref,
                 xh, bch, bcn, kva, bcv_ref, of_ref, ob_ref, bt, ct, zs, zr, fs, fr, hs, hr):
    me = lax.axis_index("seq")
    odd = lax.rem(me, 2)
    mate = me + 1 - 2 * odd
    half = n // 2
    rows = x_ref.shape[0]
    width = k_ref.shape[1]
    heads = x_ref.shape[1] // D
    nxt = lax.rem(me + 1, n)
    prv = lax.rem(me + n - 1, n)
    barrier = pltpu.get_barrier_semaphore()
    for off in range(1, n):
        pl.semaphore_signal(barrier, inc=1, **peer(seq=lax.rem(me + off, n)))
    kva[me, :, :width] = k_ref[...]
    kva[me, :, width:] = v_ref[...]
    pl.semaphore_wait(barrier, n - 1)

    def halo(slot, src, dst, to):
        return pltpu.make_async_remote_copy(
            src_ref=src, dst_ref=dst, send_sem=hs.at[slot], recv_sem=hr.at[slot], **peer(seq=to))

    last = pl.ds(rows - EDGE, EDGE)
    cx = halo(0, x_ref.at[last], xh, nxt)
    cb = halo(1, bc_ref.at[last], bch, nxt)
    cn = halo(2, bc_ref.at[pl.ds(0, EDGE)], bcn, prv)

    @pl.when(me < n - 1)
    def _():
        cb.start()
        cx.start()

    @pl.when(me > 0)
    def _():
        cn.start()

    def block(src, to, send, recv):
        return pltpu.make_async_remote_copy(
            src_ref=kva.at[src], dst_ref=kva.at[src], send_sem=send, recv_sem=recv, **peer(seq=to))

    def direct(k):
        return block(me, lax.rem(me + 2 * k, n), zs.at[k], zr.at[k])

    def arrive(k):
        return block(lax.rem(me - 2 * k + n, n), lax.rem(me + 2 * k, n), zs.at[k], zr.at[k])

    def forward(k):
        return block(lax.rem(me - 2 * k + n, n), mate, fs.at[k], fr.at[k])

    def handed(k):
        return block(lax.rem(mate - 2 * k + n, n), mate, fs.at[k], fr.at[k])

    for k in range(1, half):
        @pl.when(me + 2 * k < n)
        def _():
            direct(k).start()

    @pl.when(odd == 0)
    def _():
        forward(0).start()

    for off in range(1, n):
        @pl.when(me + off < n)
        def _():
            kva[lax.rem(me + off, n)] = jnp.zeros(kva.shape[1:], kva.dtype)

    @pl.when(me == 0)
    def _():
        xh[...] = jnp.zeros(xh.shape, xh.dtype)
        bch[...] = jnp.zeros(bch.shape, bch.dtype)

    @pl.when(me == n - 1)
    def _():
        bcn[...] = jnp.zeros(bcn.shape, bcn.dtype)

    @pl.when(me > 0)
    def _():
        cb.wait_recv()
        cx.wait_recv()

    pre = conv(bc_ref[...].astype(F32), bch[...].astype(F32), wbc_ref[...].astype(F32))
    act = (pre * sigmoid(pre)).astype(BF16)
    bcv_ref[...] = act
    act = act.astype(F32)
    bt[...] = jnp.transpose(act[:, :D]).astype(BF16)
    ct[...] = jnp.transpose(act[:, D:]).astype(BF16)

    def head(h, carry):
        lanes = pl.ds(pl.multiple_of(h * D, D), D)
        pre = conv(x_ref[:, lanes].astype(F32), xh[:, lanes].astype(F32), w_ref[:, lanes].astype(F32))
        xc = (pre * sigmoid(pre)).astype(BF16).astype(F32)
        row = run_ref[h]
        col = columns(row)
        final = row[:, rows - 1:]
        of_ref[h] = mm(bt[...], (xc * jnp.exp(final - col)).astype(BF16))
        ob_ref[h] = mm(ct[...], (dm_ref[:, lanes].astype(F32) * jnp.exp(col)).astype(BF16))
        return carry

    done = 0
    for k in range(1, half):
        upto = heads * k // half
        lax.fori_loop(done, upto, head, 0)
        done = upto

        @pl.when(me - 2 * k >= 0)
        def _():
            arrive(k).wait_recv()
            forward(k).start()

    lax.fori_loop(done, heads, head, 0)

    @pl.when(me < n - 1)
    def _():
        cb.wait_send()
        cx.wait_send()
        cn.wait_recv()

    @pl.when(me > 0)
    def _():
        cn.wait_send()

    @pl.when(odd == 0)
    def _():
        forward(0).wait_send()

    @pl.when(odd == 1)
    def _():
        handed(0).wait_recv()

    for k in range(1, half):
        @pl.when(me + 2 * k < n)
        def _():
            direct(k).wait_send()

        @pl.when(me - 2 * k >= 0)
        def _():
            forward(k).wait_send()

        @pl.when(mate - 2 * k >= 0)
        def _():
            handed(k).wait_recv()


def first_part(n, x_in, bc, keys, values, conv_x, conv_bc, run_rows, d_mixed):
    rows, width = keys.shape
    heads = x_in.shape[1] // D
    dma = pltpu.SemaphoreType.DMA
    shape = jax.ShapeDtypeStruct
    return pl.pallas_call(
        functools.partial(first_kernel, n),
        out_shape=(
            shape((EDGE, x_in.shape[1]), BF16), shape((EDGE, bc.shape[1]), BF16),
            shape((EDGE, bc.shape[1]), BF16), shape((n, rows, 2 * width), BF16),
            shape(bc.shape, BF16), shape((heads, D, D), F32), shape((heads, D, D), F32),
        ),
        in_specs=[VMEM] * 8,
        out_specs=(VMEM,) * 7,
        scratch_shapes=[pltpu.VMEM((D, rows), BF16), pltpu.VMEM((D, rows), BF16),
                        dma((n // 2,)), dma((n // 2,)), dma((n // 2,)), dma((n // 2,)),
                        dma((3,)), dma((3,))],
        compiler_params=pltpu.CompilerParams(
            collective_id=0, has_side_effects=True, vmem_limit_bytes=40 * 2**20),
        name="first",
    )(x_in, bc, keys, values, conv_x, conv_bc, run_rows, d_mixed)


def chain_kernel(n, size, of, ob, dec, kva, q_ref, dm_ref,
                 s_in, g_in, att_ref, dq_ref, dk_out, dv_out,
                 sf, sb, kt, vt, dka, dva, part, land, fs, fr, bs, br, ps, pr):
    me = lax.axis_index("seq")
    chunks = of.shape[0] // size
    rows, wide = q_ref.shape
    heads = wide // D
    kv_heads = kva.shape[2] // (2 * D)
    ratio = heads // kv_heads
    length = n * rows
    nxt = lax.rem(me + 1, n)
    prv = lax.rem(me + n - 1, n)
    barrier = pltpu.get_barrier_semaphore()
    for off in range(1, n):
        pl.semaphore_signal(barrier, inc=1, **peer(seq=lax.rem(me + off, n)))
    pl.semaphore_wait(barrier, n - 1)

    def copy(stage, landing, send, recv, c, to):
        piece = pl.ds(c * size, size)
        return pltpu.make_async_remote_copy(
            src_ref=stage.at[piece], dst_ref=landing.at[piece], send_sem=send.at[c],
            recv_sem=recv.at[c], **peer(seq=to))

    def hop(c, own, landing, stage, send, recv, to, first, last):
        piece = pl.ds(c * size, size)

        @pl.when(first)
        def _():
            landing[piece] = jnp.zeros((size,) + landing.shape[1:], landing.dtype)
            stage[piece] = own[piece].astype(BF16)

        @pl.when(jnp.logical_not(first))
        def _():
            copy(stage, landing, send, recv, c, to).wait_recv()

            @pl.when(jnp.logical_not(last))
            def _():
                stage[piece] = (dec[piece] * landing[piece].astype(F32) + own[piece]).astype(BF16)

        @pl.when(jnp.logical_not(last))
        def _():
            copy(stage, landing, send, recv, c, to).start()

    def lend(kv, off, to):
        return pltpu.make_async_remote_copy(
            src_ref=part.at[kv, to], dst_ref=land.at[kv, off], send_sem=ps.at[kv, off],
            recv_sem=pr.at[kv, off], **peer(seq=to))

    scale = D ** (-0.5)
    upos = lax.broadcasted_iota(jnp.int32, (length, rows), 0)
    tpos = lax.broadcasted_iota(jnp.int32, (length, rows), 1)

    def attend(h):
        kv = h // ratio
        lanes = pl.ds(pl.multiple_of(h * D, D), D)
        k = kva[:, :, pl.ds(pl.multiple_of(kv * D, D), D)].reshape(length, D)
        v = kva[:, :, pl.ds(pl.multiple_of((kv_heads + kv) * D, D), D)].reshape(length, D)

        @pl.when(lax.rem(h, ratio) == 0)
        def _():
            kt[...] = jnp.transpose(k.astype(F32)).astype(BF16)
            vt[...] = jnp.transpose(v.astype(F32)).astype(BF16)
            dka[...] = jnp.zeros_like(dka)
            dva[...] = jnp.zeros_like(dva)

        q = q_ref[:, lanes]
        dm = dm_ref[:, lanes]
        s = mm_nt(k, q)
        s = jnp.where(upos <= tpos + me * rows, s * (scale * math.log2(math.e)), -1e30)
        e = jnp.exp2(s - jnp.max(s, axis=0, keepdims=True))
        p = e * (1.0 / jnp.sum(e, axis=0, keepdims=True))
        pb = p.astype(BF16)
        att_t = mm(vt[...], pb)
        att_ref[:, lanes] = jnp.transpose(att_t)
        delta = jnp.sum(jnp.transpose(dm.astype(F32)) * att_t, axis=0, keepdims=True)
        ds = (p * (mm_nt(v, dm) - delta)).astype(BF16)
        dq_ref[:, lanes] = jnp.transpose(mm(kt[...], ds)) * scale
        dka[...] += mm(ds, q)
        dva[...] += mm(pb, dm)

        @pl.when(lax.rem(h, ratio) == ratio - 1)
        def _():
            part[kv, :, :, :D] = (dka[...] * scale).astype(BF16).reshape(n, rows, D)
            part[kv, :, :, D:] = dva[...].astype(BF16).reshape(n, rows, D)
            for off in range(1, n):
                @pl.when(me - off >= 0)
                def _():
                    lend(kv, off, lax.rem(me - off + n, n)).start()

    def step(t, carry):
        f = t - me
        b = t - (n - 1 - me)

        @pl.when(jnp.logical_and(f >= 0, f < chunks))
        def _():
            hop(f, of, s_in, sf, fs, fr, nxt, me == 0, me == n - 1)

        @pl.when(jnp.logical_and(b >= 0, b < chunks))
        def _():
            hop(b, ob, g_in, sb, bs, br, prv, me == n - 1, me == 0)

        @pl.when(t < heads)
        def _():
            attend(t)

        return carry

    lax.fori_loop(0, max(n - 1 + chunks, heads), step, 0)

    def drain(c, carry):
        @pl.when(me < n - 1)
        def _():
            copy(sf, s_in, fs, fr, c, nxt).wait_send()

        @pl.when(me > 0)
        def _():
            copy(sb, g_in, bs, br, c, prv).wait_send()

        return carry

    lax.fori_loop(0, chunks, drain, 0)
    for kv in range(kv_heads):
        cols = slice(kv * D, kv * D + D)
        own = part[kv, me].astype(F32)
        dk_out[:, cols] = own[:, :D]
        dv_out[:, cols] = own[:, D:]
        for off in range(1, n):
            @pl.when(me + off < n)
            def _():
                lend(kv, off, prv).wait_recv()
                came = land[kv, off].astype(F32)
                dk_out[:, cols] += came[:, :D]
                dv_out[:, cols] += came[:, D:]

    for kv in range(kv_heads):
        for off in range(1, n):
            @pl.when(me - off >= 0)
            def _():
                lend(kv, off, lax.rem(me - off + n, n)).wait_send()


def chain(n, of, ob, dec, kva, queries, d_mixed):
    heads = of.shape[0]
    rows, wide = queries.shape
    width = kva.shape[2] // 2
    kv_heads = width // D
    size = 2 if heads % 2 == 0 else 1
    chunks = heads // size
    dma = pltpu.SemaphoreType.DMA
    shape = jax.ShapeDtypeStruct
    out = shape(of.shape, BF16)
    return pl.pallas_call(
        functools.partial(chain_kernel, n, size),
        out_shape=(out, out, shape((rows, wide), F32), shape((rows, wide), F32),
                   shape((rows, width), F32), shape((rows, width), F32)),
        in_specs=[VMEM] * 6,
        out_specs=(VMEM,) * 6,
        scratch_shapes=[
            pltpu.VMEM(of.shape, BF16), pltpu.VMEM(of.shape, BF16),
            pltpu.VMEM((D, n * rows), BF16), pltpu.VMEM((D, n * rows), BF16),
            pltpu.VMEM((n * rows, D), F32), pltpu.VMEM((n * rows, D), F32),
            pltpu.VMEM((kv_heads, n, rows, 2 * D), BF16), pltpu.VMEM((kv_heads, n, rows, 2 * D), BF16),
            dma((chunks,)), dma((chunks,)), dma((chunks,)), dma((chunks,)),
            dma((kv_heads, n)), dma((kv_heads, n))],
        compiler_params=pltpu.CompilerParams(
            collective_id=1, has_side_effects=True, vmem_limit_bytes=48 * 2**20),
        name="chain",
    )(of, ob, dec, kva, queries, d_mixed)


def ssd_kernel(heads, x_ref, xh_ref, w_ref, dm_ref, bcv_ref, run_ref, skip_ref, att_ref, s_ref, g_ref,
               mixed_ref, dx_ref, gh_ref, dla_ref, dbc_ref, inner, dinner, dbc):
    h = pl.program_id(0)
    rows = x_ref.shape[0]
    b = bcv_ref[:, :D]
    c = bcv_ref[:, D:]

    @pl.when(h == 0)
    def _():
        inner[...] = mm_nt(c, b)
        dinner[...] = jnp.zeros_like(dinner)
        dbc[...] = jnp.zeros_like(dbc)

    dm = dm_ref[...]
    dmf = dm.astype(F32)
    w = w_ref[...].astype(F32)
    pre = conv(x_ref[...].astype(F32), xh_ref[...].astype(F32), w)
    sig = sigmoid(pre)
    xb = (pre * sig).astype(BF16)
    xf = xb.astype(F32)
    row = run_ref[0]
    col = columns(row)
    final = row[:, rows - 1:]
    t_i = lax.broadcasted_iota(jnp.int32, (rows, rows), 0)
    s_i = lax.broadcasted_iota(jnp.int32, (rows, rows), 1)
    fade = jnp.exp(jnp.where(t_i >= s_i, col - row, -1e30))
    mix = inner[...] * fade
    skip = skip_ref[0]
    enter = jnp.exp(col)
    tail = jnp.exp(final - col)
    state = s_ref[0]
    grad = g_ref[0]
    carried = enter * mm(c, state)
    y = mm(mix.astype(BF16), xb) + carried + skip * xf
    mixed_ref[...] = (y + att_ref[...]).astype(BF16)
    back = tail * mm(b, grad)
    gx = mm(jnp.transpose(mix).astype(BF16), dm) + back + skip * dmf
    dmix = mm_nt(dm, xb)
    dinner[...] += dmix * fade
    dbc[:, D:] += mm_nt((enter * dmf).astype(BF16), state)
    dbc[:, :D] += mm_nt((tail * xf).astype(BF16), grad)
    dgap = dmix * mix
    away = xf * back
    net = dgap - jnp.transpose(dgap) + dmf * carried - away
    net = jnp.sum(net, axis=1, keepdims=True)
    dfinal = jnp.sum(away) + jnp.sum(
        jnp.exp(final) * jnp.sum(state.astype(F32) * grad.astype(F32), axis=0, keepdims=True))
    dla_ref[0] = jnp.sum(jnp.where(t_i >= s_i, net, 0.0), axis=0, keepdims=True) + dfinal

    g = gx * (sig * (1.0 + pre * (1.0 - sig)))
    gh_ref[...] = g[:EDGE].astype(BF16)
    width = w.shape[0]
    padded = jnp.concatenate([g, jnp.zeros((8, D), F32)], axis=0)
    total = None
    for tap in range(width):
        offset = width - 1 - tap
        term = w[tap:tap + 1] * padded[offset:offset + rows]
        total = term if total is None else total + term
    dx_ref[...] = total

    @pl.when(h == heads - 1)
    def _():
        di = dinner[...]
        dbc_ref[:, D:] = (dbc[:, D:] + mm(di.astype(BF16), b)).astype(BF16)
        dbc_ref[:, :D] = (dbc[:, :D] + mm(jnp.transpose(di).astype(BF16), c)).astype(BF16)


def ssd_part(x_in, xh, conv_x, d_mixed, bcv, run_rows, skip_rows, att, s_in, g_in):
    rows, wide = x_in.shape
    heads = wide // D
    by_head = lambda r: pl.BlockSpec((r, D), lambda h: (0, h))
    whole = lambda a: pl.BlockSpec(a.shape, lambda h: (0,) * a.ndim)
    cube = pl.BlockSpec((1, D, D), lambda h: (h, 0, 0))
    line = lambda r: pl.BlockSpec((1, 1, r), lambda h: (h, 0, 0))
    shape = jax.ShapeDtypeStruct
    return pl.pallas_call(
        functools.partial(ssd_kernel, heads),
        grid=(heads,),
        out_shape=(
            shape((rows, wide), BF16), shape((rows, wide), F32), shape((EDGE, wide), BF16),
            shape((heads, 1, rows), F32), shape(bcv.shape, BF16),
        ),
        in_specs=[by_head(rows), by_head(EDGE), by_head(conv_x.shape[0]), by_head(rows), whole(bcv),
                  line(rows), line(D), by_head(rows), cube, cube],
        out_specs=(by_head(rows), by_head(rows), by_head(EDGE), line(rows), whole(bcv)),
        scratch_shapes=[pltpu.VMEM((rows, rows), F32), pltpu.VMEM((rows, rows), F32),
                        pltpu.VMEM(bcv.shape, F32)],
        name="ssd",
    )(x_in, xh, conv_x, d_mixed, bcv, run_rows, skip_rows, att, s_in, g_in)


def sums_kernel(n, m, bc_ref, gh_ref, bc_out, bcn_out, gn_out, bb, nb, bs, br, ns, nr, hs, hr):
    me = lax.axis_index("seq")
    my = lax.axis_index("head")
    nxt = lax.rem(me + 1, n)
    prv = lax.rem(me + n - 1, n)
    barrier = pltpu.get_barrier_semaphore()
    count = 0
    for to in (nxt, prv):
        pl.semaphore_signal(barrier, inc=1, **peer(seq=to, head=my))
        count += 1
    for off in range(1, m):
        other = lax.rem(my + off, m)
        for to in (me, nxt, prv):
            pl.semaphore_signal(barrier, inc=1, **peer(seq=to, head=other))
            count += 1
    pl.semaphore_wait(barrier, count)

    def remote(src, dst, send, recv, seq, head):
        return pltpu.make_async_remote_copy(
            src_ref=src, dst_ref=dst, send_sem=send, recv_sem=recv, **peer(seq=seq, head=head))

    def across(off):
        return remote(bc_ref, bb.at[off], bs.at[off], br.at[off], me, lax.rem(my + off, m))

    def before(off):
        return remote(bc_ref.at[pl.ds(0, EDGE)], nb.at[off], ns.at[off], nr.at[off], prv,
                      lax.rem(my + off, m))

    edge = remote(gh_ref, gn_out, hs, hr, prv, my)
    for off in range(1, m):
        across(off).start()

    @pl.when(me > 0)
    def _():
        edge.start()
        for off in range(m):
            before(off).start()

    total = bc_ref[...].astype(F32)
    for off in range(1, m):
        across(off).wait_recv()
        total += bb[off].astype(F32)
    bc_out[...] = total

    @pl.when(me < n - 1)
    def _():
        edge.wait_recv()
        after = None
        for off in range(m):
            before(off).wait_recv()
            part = nb[off].astype(F32)
            after = part if after is None else after + part
        bcn_out[...] = after

    @pl.when(me == n - 1)
    def _():
        gn_out[...] = jnp.zeros(gn_out.shape, gn_out.dtype)
        bcn_out[...] = jnp.zeros(bcn_out.shape, bcn_out.dtype)

    for off in range(1, m):
        across(off).wait_send()

    @pl.when(me > 0)
    def _():
        edge.wait_send()
        for off in range(m):
            before(off).wait_send()


def sums(n, m, dbc, gh):
    dma = pltpu.SemaphoreType.DMA
    shape = jax.ShapeDtypeStruct
    return pl.pallas_call(
        functools.partial(sums_kernel, n, m),
        out_shape=(shape(dbc.shape, F32), shape((EDGE, dbc.shape[1]), F32), shape(gh.shape, BF16)),
        in_specs=[VMEM] * 2,
        out_specs=(VMEM,) * 3,
        scratch_shapes=[
            pltpu.VMEM((m,) + dbc.shape, BF16), pltpu.VMEM((m, EDGE, dbc.shape[1]), BF16),
            dma((m,)), dma((m,)), dma((m,)), dma((m,)), dma, dma],
        compiler_params=pltpu.CompilerParams(collective_id=2, has_side_effects=True),
        name="sums",
    )(dbc, gh)


def silu_slope(pre):
    s = jax.nn.sigmoid(pre)
    return s * (1.0 + pre * (1.0 - s))


def shards(n, m, x_in, bc_in, conv_x, conv_bc, log_decay, skip, queries, keys, values, d_mixed):
    rows = x_in.shape[0]
    heads = x_in.shape[1] // D
    taps = conv_x.shape[0]
    edge = taps - 1
    bc = bc_in.reshape(rows, 2 * D)
    wbc = conv_bc.reshape(taps, 2 * D)
    running = jnp.cumsum(log_decay, axis=0)
    run_rows = running.T.reshape(heads, 1, rows)
    dec = jnp.broadcast_to(jnp.exp(running[-1])[:, None, None], (heads, 1, D))
    skip_rows = jnp.broadcast_to(skip[:, None, None], (heads, 1, D))
    xh, bch, bcn, kva, bcv, of, ob = first_part(
        n, x_in, bc, keys, values, conv_x, wbc, run_rows, d_mixed)
    s_in, g_in, att, dq, d_keys, d_values = chain(n, of, ob, dec, kva, queries, d_mixed)
    mixed, dx, gh, dla, dbc = ssd_part(
        x_in, xh, conv_x, d_mixed, bcv, run_rows, skip_rows, att, s_in, g_in)
    bcs, bca, gn = sums(n, m, dbc, gh)
    wx = conv_x.astype(F32)
    gnf = jnp.concatenate([jnp.zeros((edge, gn.shape[1]), F32), gn[:edge].astype(F32)], axis=0)
    fix = sum(wx[j] * gnf[edge - j:2 * edge - j] for j in range(taps))
    d_x_in = dx.at[rows - edge:].add(fix)
    wb = wbc.astype(F32)
    full = jnp.concatenate([bch[EDGE - edge:], bc, bcn[:edge]], axis=0).astype(F32)
    pre = sum(wb[j] * full[j:j + rows + edge] for j in range(taps))
    g = jnp.concatenate([bcs, bca[:edge]], axis=0) * silu_slope(pre)
    d_bc = sum(wb[j] * g[edge - j:edge - j + rows] for j in range(taps))
    return (mixed, dq, d_keys, d_values, d_x_in, d_bc.reshape(rows, 2, D), dla.reshape(heads, rows).T)


def solution(mesh):
    n, m = mesh.shape["seq"], mesh.shape["head"]
    grid = P("seq", "head")
    part = P("seq", None, None)
    in_specs = (grid, part, P(None, "head"), P(), grid, P("head"), grid, grid, grid, grid)
    out_specs = (grid, grid, grid, grid, grid, part, grid)
    return jax.shard_map(functools.partial(shards, n, m), mesh=mesh, in_specs=in_specs,
                         out_specs=out_specs, check_vma=False)
```

```python
import functools
import math

import jax
import jax.numpy as jnp
from jax import lax
from jax.experimental import pallas as pl
from jax.experimental.pallas import tpu as pltpu
from jax.sharding import PartitionSpec as P

D = 128
EDGE = 16
F32 = jnp.float32
BF16 = jnp.bfloat16
MESH = pl.DeviceIdType.MESH
VMEM = pl.BlockSpec(memory_space=pltpu.VMEM)
ANY = pl.BlockSpec(memory_space=pl.ANY)


def mm(a, b):
    return jnp.dot(a, b, preferred_element_type=F32)


def mm_nt(a, b):
    return lax.dot_general(a, b, (((1,), (1,)), ((), ())), preferred_element_type=F32)


def sigmoid(v):
    return 1.0 / (1.0 + jnp.exp(-v))


def peer(**coords):
    return dict(device_id=coords, device_id_type=MESH)


def conv(x, halo, taps):
    width = taps.shape[0]
    rows = x.shape[0]
    full = jnp.concatenate([halo[EDGE - 8:], x], axis=0)
    total = None
    for tap in range(width):
        start = 8 - (width - 1) + tap
        term = taps[tap:tap + 1] * full[start:start + rows]
        total = term if total is None else total + term
    return total


def columns(row):
    return jnp.transpose(jnp.broadcast_to(row, (D, row.shape[1])))


def first_kernel(n, x_ref, bc_ref, k_ref, v_ref, w_ref, wbc_ref, run_ref, dm_ref, dec_ref,
                 xh, bch, bcn, kva, bcv_ref, of_ref, ob_ref, rf_ref, rb_ref, rdec_ref,
                 sf, sb, bt, ct, zs, zr, fs, fr, hs, hr, ofs, ofr, obs, obr, es, er):
    me = lax.axis_index("seq")
    odd = lax.rem(me, 2)
    mate = me + 1 - 2 * odd
    half = n // 2
    rows = x_ref.shape[0]
    width = k_ref.shape[1]
    heads = x_ref.shape[1] // D
    nxt = lax.rem(me + 1, n)
    prv = lax.rem(me + n - 1, n)
    barrier = pltpu.get_barrier_semaphore()
    for off in range(1, n):
        pl.semaphore_signal(barrier, inc=1, **peer(seq=lax.rem(me + off, n)))
    kva[me, :, :width] = k_ref[...]
    kva[me, :, width:] = v_ref[...]
    pl.semaphore_wait(barrier, n - 1)

    def halo(slot, src, dst, to):
        return pltpu.make_async_remote_copy(
            src_ref=src, dst_ref=dst, send_sem=hs.at[slot], recv_sem=hr.at[slot], **peer(seq=to))

    last = pl.ds(rows - EDGE, EDGE)
    cx = halo(0, x_ref.at[last], xh, nxt)
    cb = halo(1, bc_ref.at[last], bch, nxt)
    cn = halo(2, bc_ref.at[pl.ds(0, EDGE)], bcn, prv)

    @pl.when(me < n - 1)
    def _():
        cb.start()
        cx.start()

    @pl.when(me > 0)
    def _():
        cn.start()

    share = heads // 2
    swap = pltpu.make_async_remote_copy(
        src_ref=dec_ref.at[pl.ds((1 - odd) * share, share)], dst_ref=rdec_ref, send_sem=es,
        recv_sem=er, **peer(seq=mate))
    swap.start()

    def trade(i):
        return (
            pltpu.make_async_remote_copy(
                src_ref=sf.at[i], dst_ref=rf_ref.at[i], send_sem=ofs.at[i], recv_sem=ofr.at[i],
                **peer(seq=mate)),
            pltpu.make_async_remote_copy(
                src_ref=sb.at[i], dst_ref=rb_ref.at[i], send_sem=obs.at[i], recv_sem=obr.at[i],
                **peer(seq=mate)),
        )

    def block(src, to, send, recv):
        return pltpu.make_async_remote_copy(
            src_ref=kva.at[src], dst_ref=kva.at[src], send_sem=send, recv_sem=recv, **peer(seq=to))

    def direct(k):
        return block(me, lax.rem(me + 2 * k, n), zs.at[k], zr.at[k])

    def arrive(k):
        return block(lax.rem(me - 2 * k + n, n), lax.rem(me + 2 * k, n), zs.at[k], zr.at[k])

    def forward(k):
        return block(lax.rem(me - 2 * k + n, n), mate, fs.at[k], fr.at[k])

    def handed(k):
        return block(lax.rem(mate - 2 * k + n, n), mate, fs.at[k], fr.at[k])

    for k in range(1, half):
        @pl.when(me + 2 * k < n)
        def _():
            direct(k).start()

    @pl.when(odd == 0)
    def _():
        forward(0).start()

    for off in range(1, n):
        @pl.when(me + off < n)
        def _():
            kva[lax.rem(me + off, n)] = jnp.zeros(kva.shape[1:], kva.dtype)

    @pl.when(me == 0)
    def _():
        xh[...] = jnp.zeros(xh.shape, xh.dtype)
        bch[...] = jnp.zeros(bch.shape, bch.dtype)

    @pl.when(me == n - 1)
    def _():
        bcn[...] = jnp.zeros(bcn.shape, bcn.dtype)

    @pl.when(me > 0)
    def _():
        cb.wait_recv()
        cx.wait_recv()

    pre = conv(bc_ref[...].astype(F32), bch[...].astype(F32), wbc_ref[...].astype(F32))
    act = (pre * sigmoid(pre)).astype(BF16)
    bcv_ref[...] = act
    act = act.astype(F32)
    bt[...] = jnp.transpose(act[:, :D]).astype(BF16)
    ct[...] = jnp.transpose(act[:, D:]).astype(BF16)

    def head(i, carry):
        h = lax.rem(i + (1 - odd) * share, heads)
        lanes = pl.ds(pl.multiple_of(h * D, D), D)
        pre = conv(x_ref[:, lanes].astype(F32), xh[:, lanes].astype(F32), w_ref[:, lanes].astype(F32))
        xc = (pre * sigmoid(pre)).astype(BF16).astype(F32)
        row = run_ref[h]
        col = columns(row)
        final = row[:, rows - 1:]
        own_f = mm(bt[...], (xc * jnp.exp(final - col)).astype(BF16))
        own_b = mm(ct[...], (dm_ref[:, lanes].astype(F32) * jnp.exp(col)).astype(BF16))

        @pl.when(i < share)
        def _():
            sf[i] = own_f.astype(BF16)
            sb[i] = own_b.astype(BF16)
            for cp in trade(i):
                cp.start()

        @pl.when(i >= share)
        def _():
            of_ref[i - share] = own_f
            ob_ref[i - share] = own_b

        return carry

    done = 0
    for k in range(1, half):
        upto = heads * k // half
        lax.fori_loop(done, upto, head, 0)
        done = upto

        @pl.when(me - 2 * k >= 0)
        def _():
            arrive(k).wait_recv()
            forward(k).start()

    lax.fori_loop(done, heads, head, 0)
    swap.wait()

    def settle(i, carry):
        for cp in trade(i):
            cp.wait()
        return carry

    lax.fori_loop(0, share, settle, 0)

    @pl.when(me < n - 1)
    def _():
        cb.wait_send()
        cx.wait_send()
        cn.wait_recv()

    @pl.when(me > 0)
    def _():
        cn.wait_send()

    @pl.when(odd == 0)
    def _():
        forward(0).wait_send()

    @pl.when(odd == 1)
    def _():
        handed(0).wait_recv()

    for k in range(1, half):
        @pl.when(me + 2 * k < n)
        def _():
            direct(k).wait_send()

        @pl.when(me - 2 * k >= 0)
        def _():
            forward(k).wait_send()

        @pl.when(mate - 2 * k >= 0)
        def _():
            handed(k).wait_recv()


def first_part(n, x_in, bc, keys, values, conv_x, conv_bc, run_rows, d_mixed, dec):
    rows, width = keys.shape
    share = x_in.shape[1] // D // 2
    dma = pltpu.SemaphoreType.DMA
    shape = jax.ShapeDtypeStruct
    return pl.pallas_call(
        functools.partial(first_kernel, n),
        out_shape=(
            shape((EDGE, x_in.shape[1]), BF16), shape((EDGE, bc.shape[1]), BF16),
            shape((EDGE, bc.shape[1]), BF16), shape((n, rows, 2 * width), BF16),
            shape(bc.shape, BF16), shape((share, D, D), F32), shape((share, D, D), F32),
            shape((share, D, D), BF16), shape((share, D, D), BF16), shape((share, 1, D), F32),
        ),
        in_specs=[VMEM] * 9,
        out_specs=(VMEM,) * 10,
        scratch_shapes=[pltpu.VMEM((share, D, D), BF16), pltpu.VMEM((share, D, D), BF16),
                        pltpu.VMEM((D, rows), BF16), pltpu.VMEM((D, rows), BF16),
                        dma((n // 2,)), dma((n // 2,)), dma((n // 2,)), dma((n // 2,)),
                        dma((3,)), dma((3,)), dma((share,)), dma((share,)), dma((share,)),
                        dma((share,)), dma, dma],
        compiler_params=pltpu.CompilerParams(
            collective_id=0, has_side_effects=True, vmem_limit_bytes=20 * 2**20),
        name="first",
    )(x_in, bc, keys, values, conv_x, conv_bc, run_rows, d_mixed, dec)


def chain_kernel(n, size, of, ob, rf, rb, dec, rdec, kva, q_ref, dm_ref,
                 s_in, g_in, att_ref, dq_ref, dk_out, dv_out,
                 af, ab, sf, sb, mf, mb, kt, vt, dka, dva, part, land,
                 fs, fr, bs, br, mfs, mfr, mbs, mbr, ps, pr):
    me = lax.axis_index("seq")
    share = of.shape[0]
    chunks = share // size
    rows, wide = q_ref.shape
    heads = wide // D
    kv_heads = kva.shape[2] // (2 * D)
    ratio = heads // kv_heads
    length = n * rows
    odd = lax.rem(me, 2)
    mate = me + 1 - 2 * odd
    base = odd * share
    level = me // 2
    levels = n // 2
    up = lax.rem(me + 2, n)
    down = lax.rem(me + n - 2, n)
    prv = lax.rem(me + n - 1, n)
    barrier = pltpu.get_barrier_semaphore()
    for off in range(1, n):
        pl.semaphore_signal(barrier, inc=1, **peer(seq=lax.rem(me + off, n)))
    pl.semaphore_wait(barrier, n - 1)

    def copy(stage, landing, send, recv, c, to):
        piece = pl.ds(c * size, size)
        return pltpu.make_async_remote_copy(
            src_ref=stage.at[piece], dst_ref=landing.at[piece], send_sem=send.at[c],
            recv_sem=recv.at[c], **peer(seq=to))

    def give(stage, out, send, recv, c, start):
        return pltpu.make_async_remote_copy(
            src_ref=stage.at[pl.ds(c * size, size)], dst_ref=out.at[pl.ds(start + c * size, size)],
            send_sem=send.at[c], recv_sem=recv.at[c], **peer(seq=mate))

    is_odd = odd == 1

    def ahead(c, x):
        piece = pl.ds(c * size, size)
        mine, other = of[piece], rf[piece].astype(F32)
        even_f, odd_f = jnp.where(is_odd, other, mine), jnp.where(is_odd, mine, other)
        even_d = jnp.where(is_odd, rdec[piece], dec[pl.ds(base + c * size, size)])
        odd_d = jnp.where(is_odd, dec[pl.ds(base + c * size, size)], rdec[piece])
        middle = even_d * x + even_f
        return jnp.where(is_odd, middle, x), jnp.where(is_odd, x, middle), odd_d * middle + odd_f

    def behind(c, x):
        piece = pl.ds(c * size, size)
        mine, other = ob[piece], rb[piece].astype(F32)
        even_b, odd_b = jnp.where(is_odd, other, mine), jnp.where(is_odd, mine, other)
        even_d = jnp.where(is_odd, rdec[piece], dec[pl.ds(base + c * size, size)])
        odd_d = jnp.where(is_odd, dec[pl.ds(base + c * size, size)], rdec[piece])
        middle = odd_d * x + odd_b
        return jnp.where(is_odd, x, middle), jnp.where(is_odd, middle, x), even_d * middle + even_b

    def hop(c, join, landing, stage, send, recv, to, first, last, out, gift, gsend, grecv):
        piece = pl.ds(c * size, size)

        @pl.when(first)
        def _():
            landing[piece] = jnp.zeros((size,) + landing.shape[1:], landing.dtype)

        @pl.when(jnp.logical_not(first))
        def _():
            copy(stage, landing, send, recv, c, to).wait_recv()

        mine, other, on = join(c, landing[piece].astype(F32))
        stage[piece] = on.astype(BF16)

        @pl.when(jnp.logical_not(last))
        def _():
            copy(stage, landing, send, recv, c, to).start()

        out[pl.ds(base + c * size, size)] = mine.astype(BF16)
        gift[piece] = other.astype(BF16)
        give(gift, out, gsend, grecv, c, base).start()

    def lend(kv, off, to):
        return pltpu.make_async_remote_copy(
            src_ref=part.at[kv, to], dst_ref=land.at[kv, off], send_sem=ps.at[kv, off],
            recv_sem=pr.at[kv, off], **peer(seq=to))

    scale = D ** (-0.5)
    upos = lax.broadcasted_iota(jnp.int32, (length, rows), 0)
    tpos = lax.broadcasted_iota(jnp.int32, (length, rows), 1)

    def attend(h):
        kv = h // ratio
        lanes = pl.ds(pl.multiple_of(h * D, D), D)
        k = kva[:, :, pl.ds(pl.multiple_of(kv * D, D), D)].reshape(length, D)
        v = kva[:, :, pl.ds(pl.multiple_of((kv_heads + kv) * D, D), D)].reshape(length, D)

        @pl.when(lax.rem(h, ratio) == 0)
        def _():
            kt[...] = jnp.transpose(k.astype(F32)).astype(BF16)
            vt[...] = jnp.transpose(v.astype(F32)).astype(BF16)
            dka[...] = jnp.zeros_like(dka)
            dva[...] = jnp.zeros_like(dva)

        q = q_ref[:, lanes]
        dm = dm_ref[:, lanes]
        s = mm_nt(k, q)
        s = jnp.where(upos <= tpos + me * rows, s * (scale * math.log2(math.e)), -1e30)
        e = jnp.exp2(s - jnp.max(s, axis=0, keepdims=True))
        p = e * (1.0 / jnp.sum(e, axis=0, keepdims=True))
        pb = p.astype(BF16)
        att_t = mm(vt[...], pb)
        att_ref[:, lanes] = jnp.transpose(att_t)
        delta = jnp.sum(jnp.transpose(dm.astype(F32)) * att_t, axis=0, keepdims=True)
        ds = (p * (mm_nt(v, dm) - delta)).astype(BF16)
        dq_ref[:, lanes] = jnp.transpose(mm(kt[...], ds)) * scale
        dka[...] += mm(ds, q)
        dva[...] += mm(pb, dm)

        @pl.when(lax.rem(h, ratio) == ratio - 1)
        def _():
            part[kv, :, :, :D] = (dka[...] * scale).astype(BF16).reshape(n, rows, D)
            part[kv, :, :, D:] = dva[...].astype(BF16).reshape(n, rows, D)
            for off in range(1, n):
                @pl.when(me - off >= 0)
                def _():
                    lend(kv, off, lax.rem(me - off + n, n)).start()

    def step(t, carry):
        f = t - level
        b = t - (levels - 1 - level)

        @pl.when(jnp.logical_and(f >= 0, f < chunks))
        def _():
            hop(f, ahead, af, sf, fs, fr, up, level == 0, level == levels - 1,
                s_in, mf, mfs, mfr)

        @pl.when(jnp.logical_and(b >= 0, b < chunks))
        def _():
            hop(b, behind, ab, sb, bs, br, down, level == levels - 1, level == 0,
                g_in, mb, mbs, mbr)

        @pl.when(t < heads)
        def _():
            attend(t)

        return carry

    lax.fori_loop(0, max(levels - 1 + chunks, heads), step, 0)

    def drain(c, carry):
        @pl.when(level < levels - 1)
        def _():
            copy(sf, af, fs, fr, c, up).wait_send()

        @pl.when(level > 0)
        def _():
            copy(sb, ab, bs, br, c, down).wait_send()

        give(mf, s_in, mfs, mfr, c, base).wait_send()
        give(mb, g_in, mbs, mbr, c, base).wait_send()
        give(mf, s_in, mfs, mfr, c, share - base).wait_recv()
        give(mb, g_in, mbs, mbr, c, share - base).wait_recv()

        return carry

    lax.fori_loop(0, chunks, drain, 0)
    for kv in range(kv_heads):
        cols = slice(kv * D, kv * D + D)
        own = part[kv, me].astype(F32)
        dk_out[:, cols] = own[:, :D]
        dv_out[:, cols] = own[:, D:]
        for off in range(1, n):
            @pl.when(me + off < n)
            def _():
                lend(kv, off, prv).wait_recv()
                came = land[kv, off].astype(F32)
                dk_out[:, cols] += came[:, :D]
                dv_out[:, cols] += came[:, D:]

    for kv in range(kv_heads):
        for off in range(1, n):
            @pl.when(me - off >= 0)
            def _():
                lend(kv, off, lax.rem(me - off + n, n)).wait_send()


def chain(n, of, ob, rf, rb, dec, rdec, kva, queries, d_mixed):
    share = of.shape[0]
    rows, wide = queries.shape
    width = kva.shape[2] // 2
    kv_heads = width // D
    size = 2 if share % 2 == 0 else 1
    chunks = share // size
    dma = pltpu.SemaphoreType.DMA
    shape = jax.ShapeDtypeStruct
    out = shape((2 * share, D, D), BF16)
    return pl.pallas_call(
        functools.partial(chain_kernel, n, size),
        out_shape=(out, out, shape((rows, wide), F32), shape((rows, wide), F32),
                   shape((rows, width), F32), shape((rows, width), F32)),
        in_specs=[VMEM] * 9,
        out_specs=(VMEM,) * 6,
        scratch_shapes=[
            *[pltpu.VMEM(of.shape, BF16) for _ in range(6)],
            pltpu.VMEM((D, n * rows), BF16), pltpu.VMEM((D, n * rows), BF16),
            pltpu.VMEM((n * rows, D), F32), pltpu.VMEM((n * rows, D), F32),
            pltpu.VMEM((kv_heads, n, rows, 2 * D), BF16), pltpu.VMEM((kv_heads, n, rows, 2 * D), BF16),
            *[dma((chunks,)) for _ in range(8)],
            dma((kv_heads, n)), dma((kv_heads, n))],
        compiler_params=pltpu.CompilerParams(
            collective_id=1, has_side_effects=True, vmem_limit_bytes=28 * 2**20),
        name="chain",
    )(of, ob, rf, rb, dec, rdec, kva, queries, d_mixed)


def ssd_kernel(heads, x_ref, xh_ref, w_ref, dm_ref, bcv_ref, run_ref, skip_ref, att_ref, s_ref, g_ref,
               dqi_ref, dki_ref, dvi_ref, mixed_ref, dx_ref, gh_ref, dla_ref, dbc_ref,
               dq_ref, dk_ref, dv_ref, inner, dinner, dbc):
    h = pl.program_id(0)
    rows = x_ref.shape[0]
    b = bcv_ref[:, :D]
    c = bcv_ref[:, D:]

    @pl.when(h == 0)
    def _():
        inner[...] = mm_nt(c, b)
        dinner[...] = jnp.zeros_like(dinner)
        dbc[...] = jnp.zeros_like(dbc)

    dq_ref[...] = dqi_ref[...]
    dm = dm_ref[...]
    dmf = dm.astype(F32)
    w = w_ref[...].astype(F32)
    pre = conv(x_ref[...].astype(F32), xh_ref[...].astype(F32), w)
    sig = sigmoid(pre)
    xb = (pre * sig).astype(BF16)
    xf = xb.astype(F32)
    row = run_ref[0]
    col = columns(row)
    final = row[:, rows - 1:]
    t_i = lax.broadcasted_iota(jnp.int32, (rows, rows), 0)
    s_i = lax.broadcasted_iota(jnp.int32, (rows, rows), 1)
    fade = jnp.exp(jnp.where(t_i >= s_i, col - row, -1e30))
    mix = inner[...] * fade
    skip = skip_ref[0]
    enter = jnp.exp(col)
    tail = jnp.exp(final - col)
    state = s_ref[0]
    grad = g_ref[0]
    carried = enter * mm(c, state)
    y = mm(mix.astype(BF16), xb) + carried + skip * xf
    mixed_ref[...] = (y + att_ref[...]).astype(BF16)
    back = tail * mm(b, grad)
    gx = mm(jnp.transpose(mix).astype(BF16), dm) + back + skip * dmf
    dmix = mm_nt(dm, xb)
    dinner[...] += dmix * fade
    dbc[:, D:] += mm_nt((enter * dmf).astype(BF16), state)
    dbc[:, :D] += mm_nt((tail * xf).astype(BF16), grad)
    dgap = dmix * mix
    away = xf * back
    net = dgap - jnp.transpose(dgap) + dmf * carried - away
    net = jnp.sum(net, axis=1, keepdims=True)
    dfinal = jnp.sum(away) + jnp.sum(
        jnp.exp(final) * jnp.sum(state.astype(F32) * grad.astype(F32), axis=0, keepdims=True))
    dla_ref[0] = jnp.sum(jnp.where(t_i >= s_i, net, 0.0), axis=0, keepdims=True) + dfinal

    g = gx * (sig * (1.0 + pre * (1.0 - sig)))
    gh_ref[...] = g[:EDGE].astype(BF16)
    width = w.shape[0]
    padded = jnp.concatenate([g, jnp.zeros((8, D), F32)], axis=0)
    total = None
    for tap in range(width):
        offset = width - 1 - tap
        term = w[tap:tap + 1] * padded[offset:offset + rows]
        total = term if total is None else total + term
    dx_ref[...] = total

    @pl.when(h == heads - 1)
    def _():
        dk_ref[...] = dki_ref[...]
        dv_ref[...] = dvi_ref[...]
        di = dinner[...]
        dbc_ref[:, D:] = (dbc[:, D:] + mm(di.astype(BF16), b)).astype(BF16)
        dbc_ref[:, :D] = (dbc[:, :D] + mm(jnp.transpose(di).astype(BF16), c)).astype(BF16)


def ssd_part(x_in, xh, conv_x, d_mixed, bcv, run_rows, skip_rows, att, s_in, g_in, dq, dk, dv):
    rows, wide = x_in.shape
    heads = wide // D
    by_head = lambda r: pl.BlockSpec((r, D), lambda h: (0, h))
    whole = lambda a: pl.BlockSpec(a.shape, lambda h: (0,) * a.ndim)
    cube = pl.BlockSpec((1, D, D), lambda h: (h, 0, 0))
    line = lambda r: pl.BlockSpec((1, 1, r), lambda h: (h, 0, 0))
    shape = jax.ShapeDtypeStruct
    return pl.pallas_call(
        functools.partial(ssd_kernel, heads),
        grid=(heads,),
        out_shape=(
            shape((rows, wide), BF16), shape((rows, wide), F32), shape((EDGE, wide), BF16),
            shape((heads, 1, rows), F32), shape(bcv.shape, BF16), shape((rows, wide), F32),
            shape(dk.shape, F32), shape(dv.shape, F32),
        ),
        in_specs=[by_head(rows), by_head(EDGE), by_head(conv_x.shape[0]), by_head(rows), whole(bcv),
                  line(rows), line(D), by_head(rows), cube, cube, by_head(rows), whole(dk),
                  whole(dv)],
        out_specs=(by_head(rows), by_head(rows), by_head(EDGE), line(rows), whole(bcv),
                   by_head(rows), whole(dk), whole(dv)),
        scratch_shapes=[pltpu.VMEM((rows, rows), F32), pltpu.VMEM((rows, rows), F32),
                        pltpu.VMEM(bcv.shape, F32)],
        name="ssd",
    )(x_in, xh, conv_x, d_mixed, bcv, run_rows, skip_rows, att, s_in, g_in, dq, dk, dv)


def sums_kernel(n, m, bc_ref, gh_ref, bc_out, bcn_out, gn_out, bb, nb, bs, br, ns, nr, hs, hr):
    me = lax.axis_index("seq")
    my = lax.axis_index("head")
    nxt = lax.rem(me + 1, n)
    prv = lax.rem(me + n - 1, n)
    barrier = pltpu.get_barrier_semaphore()
    count = 0
    for to in (nxt, prv):
        pl.semaphore_signal(barrier, inc=1, **peer(seq=to, head=my))
        count += 1
    for off in range(1, m):
        other = lax.rem(my + off, m)
        for to in (me, nxt, prv):
            pl.semaphore_signal(barrier, inc=1, **peer(seq=to, head=other))
            count += 1
    pl.semaphore_wait(barrier, count)

    def remote(src, dst, send, recv, seq, head):
        return pltpu.make_async_remote_copy(
            src_ref=src, dst_ref=dst, send_sem=send, recv_sem=recv, **peer(seq=seq, head=head))

    def across(off):
        return remote(bc_ref, bb.at[off], bs.at[off], br.at[off], me, lax.rem(my + off, m))

    def before(off):
        return remote(bc_ref.at[pl.ds(0, EDGE)], nb.at[off], ns.at[off], nr.at[off], prv,
                      lax.rem(my + off, m))

    edge = remote(gh_ref, gn_out, hs, hr, prv, my)
    for off in range(1, m):
        across(off).start()

    @pl.when(me > 0)
    def _():
        edge.start()
        for off in range(m):
            before(off).start()

    total = bc_ref[...].astype(F32)
    for off in range(1, m):
        across(off).wait_recv()
        total += bb[off].astype(F32)
    bc_out[...] = total

    @pl.when(me < n - 1)
    def _():
        edge.wait_recv()
        after = None
        for off in range(m):
            before(off).wait_recv()
            part = nb[off].astype(F32)
            after = part if after is None else after + part
        bcn_out[...] = after

    @pl.when(me == n - 1)
    def _():
        gn_out[...] = jnp.zeros(gn_out.shape, gn_out.dtype)
        bcn_out[...] = jnp.zeros(bcn_out.shape, bcn_out.dtype)

    for off in range(1, m):
        across(off).wait_send()

    @pl.when(me > 0)
    def _():
        edge.wait_send()
        for off in range(m):
            before(off).wait_send()


def sums(n, m, dbc, gh):
    dma = pltpu.SemaphoreType.DMA
    shape = jax.ShapeDtypeStruct
    return pl.pallas_call(
        functools.partial(sums_kernel, n, m),
        out_shape=(shape(dbc.shape, F32), shape((EDGE, dbc.shape[1]), F32), shape(gh.shape, BF16)),
        in_specs=[VMEM] * 2,
        out_specs=(VMEM,) * 3,
        scratch_shapes=[
            pltpu.VMEM((m,) + dbc.shape, BF16), pltpu.VMEM((m, EDGE, dbc.shape[1]), BF16),
            dma((m,)), dma((m,)), dma((m,)), dma((m,)), dma, dma],
        compiler_params=pltpu.CompilerParams(collective_id=2, has_side_effects=True),
        name="sums",
    )(dbc, gh)


def silu_slope(pre):
    s = jax.nn.sigmoid(pre)
    return s * (1.0 + pre * (1.0 - s))


def shards(n, m, x_in, bc_in, conv_x, conv_bc, log_decay, skip, queries, keys, values, d_mixed):
    rows = x_in.shape[0]
    heads = x_in.shape[1] // D
    taps = conv_x.shape[0]
    edge = taps - 1
    bc = bc_in.reshape(rows, 2 * D)
    wbc = conv_bc.reshape(taps, 2 * D)
    running = jnp.cumsum(log_decay, axis=0)
    run_rows = running.T.reshape(heads, 1, rows)
    dec = jnp.broadcast_to(jnp.exp(running[-1])[:, None, None], (heads, 1, D))
    skip_rows = jnp.broadcast_to(skip[:, None, None], (heads, 1, D))
    xh, bch, bcn, kva, bcv, of, ob, rf, rb, rdec = first_part(
        n, x_in, bc, keys, values, conv_x, wbc, run_rows, d_mixed, dec)
    s_in, g_in, att, dq, dk, dv = chain(n, of, ob, rf, rb, dec, rdec, kva, queries, d_mixed)
    mixed, dx, gh, dla, dbc, dq, d_keys, d_values = ssd_part(
        x_in, xh, conv_x, d_mixed, bcv, run_rows, skip_rows, att, s_in, g_in, dq, dk, dv)
    bcs, bca, gn = sums(n, m, dbc, gh)
    wx = conv_x.astype(F32)
    gnf = jnp.concatenate([jnp.zeros((edge, gn.shape[1]), F32), gn[:edge].astype(F32)], axis=0)
    fix = sum(wx[j] * gnf[edge - j:2 * edge - j] for j in range(taps))
    d_x_in = dx.at[rows - edge:].add(fix)
    wb = wbc.astype(F32)
    full = jnp.concatenate([bch[EDGE - edge:], bc, bcn[:edge]], axis=0).astype(F32)
    pre = sum(wb[j] * full[j:j + rows + edge] for j in range(taps))
    g = jnp.concatenate([bcs, bca[:edge]], axis=0) * silu_slope(pre)
    d_bc = sum(wb[j] * g[edge - j:edge - j + rows] for j in range(taps))
    return (mixed, dq, d_keys, d_values, d_x_in, d_bc.reshape(rows, 2, D), dla.reshape(heads, rows).T)


def solution(mesh):
    n, m = mesh.shape["seq"], mesh.shape["head"]
    grid = P("seq", "head")
    part = P("seq", None, None)
    in_specs = (grid, part, P(None, "head"), P(), grid, P("head"), grid, grid, grid, grid)
    out_specs = (grid, grid, grid, grid, grid, part, grid)
    return jax.shard_map(functools.partial(shards, n, m), mesh=mesh, in_specs=in_specs,
                         out_specs=out_specs, check_vma=False)
```

```python
import functools
import math

import jax
import jax.numpy as jnp
from jax import lax
from jax.experimental import pallas as pl
from jax.experimental.pallas import tpu as pltpu
from jax.sharding import PartitionSpec as P

D = 128
EDGE = 16
F32 = jnp.float32
BF16 = jnp.bfloat16
MESH = pl.DeviceIdType.MESH
VMEM = pl.BlockSpec(memory_space=pltpu.VMEM)
ANY = pl.BlockSpec(memory_space=pl.ANY)


def mm(a, b):
    return jnp.dot(a, b, preferred_element_type=F32)


def mm_nt(a, b):
    return lax.dot_general(a, b, (((1,), (1,)), ((), ())), preferred_element_type=F32)


def sigmoid(v):
    return 1.0 / (1.0 + jnp.exp(-v))


def peer(**coords):
    return dict(device_id=coords, device_id_type=MESH)


def conv(x, halo, taps):
    width = taps.shape[0]
    rows = x.shape[0]
    full = jnp.concatenate([halo[EDGE - 8:], x], axis=0)
    total = None
    for tap in range(width):
        start = 8 - (width - 1) + tap
        term = taps[tap:tap + 1] * full[start:start + rows]
        total = term if total is None else total + term
    return total


def columns(row):
    return jnp.transpose(jnp.broadcast_to(row, (D, row.shape[1])))


def first_kernel(n, x_ref, bc_ref, k_ref, v_ref, w_ref, wbc_ref, run_ref, dm_ref, dec_ref,
                 xh, bch, bcn, kva, bcv_ref, of_ref, ob_ref, rf_ref, rb_ref, rdec_ref,
                 sf, sb, bt, ct, zs, zr, fs, fr, hs, hr, ofs, ofr, obs, obr, es, er):
    me = lax.axis_index("seq")
    odd = lax.rem(me, 2)
    mate = me + 1 - 2 * odd
    half = n // 2
    rows = x_ref.shape[0]
    width = k_ref.shape[1]
    heads = x_ref.shape[1] // D
    nxt = lax.rem(me + 1, n)
    prv = lax.rem(me + n - 1, n)
    barrier = pltpu.get_barrier_semaphore()
    for off in range(1, n):
        pl.semaphore_signal(barrier, inc=1, **peer(seq=lax.rem(me + off, n)))
    kva[me, :, :width] = k_ref[...]
    kva[me, :, width:] = v_ref[...]
    pl.semaphore_wait(barrier, n - 1)

    def halo(slot, src, dst, to):
        return pltpu.make_async_remote_copy(
            src_ref=src, dst_ref=dst, send_sem=hs.at[slot], recv_sem=hr.at[slot], **peer(seq=to))

    last = pl.ds(rows - EDGE, EDGE)
    cx = halo(0, x_ref.at[last], xh, nxt)
    cb = halo(1, bc_ref.at[last], bch, nxt)
    cn = halo(2, bc_ref.at[pl.ds(0, EDGE)], bcn, prv)

    @pl.when(me < n - 1)
    def _():
        cb.start()
        cx.start()

    @pl.when(me > 0)
    def _():
        cn.start()

    share = heads // 2
    swap = pltpu.make_async_remote_copy(
        src_ref=dec_ref.at[pl.ds((1 - odd) * share, share)], dst_ref=rdec_ref, send_sem=es,
        recv_sem=er, **peer(seq=mate))
    swap.start()

    def trade(i):
        return (
            pltpu.make_async_remote_copy(
                src_ref=sf.at[i], dst_ref=rf_ref.at[i], send_sem=ofs.at[i], recv_sem=ofr.at[i],
                **peer(seq=mate)),
            pltpu.make_async_remote_copy(
                src_ref=sb.at[i], dst_ref=rb_ref.at[i], send_sem=obs.at[i], recv_sem=obr.at[i],
                **peer(seq=mate)),
        )

    def block(src, to, send, recv):
        return pltpu.make_async_remote_copy(
            src_ref=kva.at[src], dst_ref=kva.at[src], send_sem=send, recv_sem=recv, **peer(seq=to))

    def direct(k):
        return block(me, lax.rem(me + 2 * k, n), zs.at[k], zr.at[k])

    def arrive(k):
        return block(lax.rem(me - 2 * k + n, n), lax.rem(me + 2 * k, n), zs.at[k], zr.at[k])

    def forward(k):
        return block(lax.rem(me - 2 * k + n, n), mate, fs.at[k], fr.at[k])

    def handed(k):
        return block(lax.rem(mate - 2 * k + n, n), mate, fs.at[k], fr.at[k])

    for k in range(1, half):
        @pl.when(me + 2 * k < n)
        def _():
            direct(k).start()

    @pl.when(odd == 0)
    def _():
        forward(0).start()

    for off in range(1, n):
        @pl.when(me + off < n)
        def _():
            kva[lax.rem(me + off, n)] = jnp.zeros(kva.shape[1:], kva.dtype)

    @pl.when(me == 0)
    def _():
        xh[...] = jnp.zeros(xh.shape, xh.dtype)
        bch[...] = jnp.zeros(bch.shape, bch.dtype)

    @pl.when(me == n - 1)
    def _():
        bcn[...] = jnp.zeros(bcn.shape, bcn.dtype)

    @pl.when(me > 0)
    def _():
        cb.wait_recv()
        cx.wait_recv()

    pre = conv(bc_ref[...].astype(F32), bch[...].astype(F32), wbc_ref[...].astype(F32))
    act = (pre * sigmoid(pre)).astype(BF16)
    bcv_ref[...] = act
    act = act.astype(F32)
    bt[...] = jnp.transpose(act[:, :D]).astype(BF16)
    ct[...] = jnp.transpose(act[:, D:]).astype(BF16)

    def head(i, carry):
        h = lax.rem(i + (1 - odd) * share, heads)
        lanes = pl.ds(pl.multiple_of(h * D, D), D)
        pre = conv(x_ref[:, lanes].astype(F32), xh[:, lanes].astype(F32), w_ref[:, lanes].astype(F32))
        xc = (pre * sigmoid(pre)).astype(BF16).astype(F32)
        row = run_ref[h]
        col = columns(row)
        final = row[:, rows - 1:]
        own_f = mm(bt[...], (xc * jnp.exp(final - col)).astype(BF16))
        own_b = mm(ct[...], (dm_ref[:, lanes].astype(F32) * jnp.exp(col)).astype(BF16))

        @pl.when(i < share)
        def _():
            sf[i] = own_f.astype(BF16)
            sb[i] = own_b.astype(BF16)
            for cp in trade(i):
                cp.start()

        @pl.when(i >= share)
        def _():
            of_ref[i - share] = own_f
            ob_ref[i - share] = own_b

        return carry

    done = 0
    for k in range(1, half):
        upto = heads * k // half
        lax.fori_loop(done, upto, head, 0)
        done = upto

        @pl.when(me - 2 * k >= 0)
        def _():
            arrive(k).wait_recv()
            forward(k).start()

    lax.fori_loop(done, heads, head, 0)
    swap.wait()

    def settle(i, carry):
        for cp in trade(i):
            cp.wait()
        return carry

    lax.fori_loop(0, share, settle, 0)

    @pl.when(me < n - 1)
    def _():
        cb.wait_send()
        cx.wait_send()
        cn.wait_recv()

    @pl.when(me > 0)
    def _():
        cn.wait_send()

    @pl.when(odd == 0)
    def _():
        forward(0).wait_send()

    @pl.when(odd == 1)
    def _():
        handed(0).wait_recv()

    for k in range(1, half):
        @pl.when(me + 2 * k < n)
        def _():
            direct(k).wait_send()

        @pl.when(me - 2 * k >= 0)
        def _():
            forward(k).wait_send()

        @pl.when(mate - 2 * k >= 0)
        def _():
            handed(k).wait_recv()


def first_part(n, x_in, bc, keys, values, conv_x, conv_bc, run_rows, d_mixed, dec):
    rows, width = keys.shape
    share = x_in.shape[1] // D // 2
    dma = pltpu.SemaphoreType.DMA
    shape = jax.ShapeDtypeStruct
    return pl.pallas_call(
        functools.partial(first_kernel, n),
        out_shape=(
            shape((EDGE, x_in.shape[1]), BF16), shape((EDGE, bc.shape[1]), BF16),
            shape((EDGE, bc.shape[1]), BF16), shape((n, rows, 2 * width), BF16),
            shape(bc.shape, BF16), shape((share, D, D), F32), shape((share, D, D), F32),
            shape((share, D, D), BF16), shape((share, D, D), BF16), shape((share, 1, D), F32),
        ),
        in_specs=[VMEM] * 9,
        out_specs=(VMEM,) * 10,
        scratch_shapes=[pltpu.VMEM((share, D, D), BF16), pltpu.VMEM((share, D, D), BF16),
                        pltpu.VMEM((D, rows), BF16), pltpu.VMEM((D, rows), BF16),
                        dma((n // 2,)), dma((n // 2,)), dma((n // 2,)), dma((n // 2,)),
                        dma((3,)), dma((3,)), dma((share,)), dma((share,)), dma((share,)),
                        dma((share,)), dma, dma],
        compiler_params=pltpu.CompilerParams(
            collective_id=0, has_side_effects=True, vmem_limit_bytes=20 * 2**20),
        name="first",
    )(x_in, bc, keys, values, conv_x, conv_bc, run_rows, d_mixed, dec)


def chain_kernel(n, size, of, ob, rf, rb, dec, rdec, kva, q_ref, dm_ref,
                 x_ref, xh_ref, w_ref, bcv_ref, run_ref, skip_ref,
                 dq_ref, dk_out, dv_out, mixed_ref, dx_ref, gh_ref, dla_ref, dbc_ref,
                 s_in, g_in, att_ref, inner, dinner, dbc, af, ab, sf, sb, mf, mb, kt, vt, dka, dva, part, land,
                 fs, fr, bs, br, mfs, mfr, mbs, mbr, ps, pr):
    me = lax.axis_index("seq")
    share = of.shape[0]
    chunks = share // size
    rows, wide = q_ref.shape
    heads = wide // D
    kv_heads = kva.shape[2] // (2 * D)
    ratio = heads // kv_heads
    length = n * rows
    odd = lax.rem(me, 2)
    mate = me + 1 - 2 * odd
    base = odd * share
    level = me // 2
    levels = n // 2
    up = lax.rem(me + 2, n)
    down = lax.rem(me + n - 2, n)
    prv = lax.rem(me + n - 1, n)
    barrier = pltpu.get_barrier_semaphore()
    for off in range(1, n):
        pl.semaphore_signal(barrier, inc=1, **peer(seq=lax.rem(me + off, n)))
    pl.semaphore_wait(barrier, n - 1)

    def copy(stage, landing, send, recv, c, to):
        piece = pl.ds(c * size, size)
        return pltpu.make_async_remote_copy(
            src_ref=stage.at[piece], dst_ref=landing.at[piece], send_sem=send.at[c],
            recv_sem=recv.at[c], **peer(seq=to))

    def give(stage, out, send, recv, c, start):
        return pltpu.make_async_remote_copy(
            src_ref=stage.at[pl.ds(c * size, size)], dst_ref=out.at[pl.ds(start + c * size, size)],
            send_sem=send.at[c], recv_sem=recv.at[c], **peer(seq=mate))

    is_odd = odd == 1

    def ahead(c, x):
        piece = pl.ds(c * size, size)
        mine, other = of[piece], rf[piece].astype(F32)
        even_f, odd_f = jnp.where(is_odd, other, mine), jnp.where(is_odd, mine, other)
        even_d = jnp.where(is_odd, rdec[piece], dec[pl.ds(base + c * size, size)])
        odd_d = jnp.where(is_odd, dec[pl.ds(base + c * size, size)], rdec[piece])
        middle = even_d * x + even_f
        return jnp.where(is_odd, middle, x), jnp.where(is_odd, x, middle), odd_d * middle + odd_f

    def behind(c, x):
        piece = pl.ds(c * size, size)
        mine, other = ob[piece], rb[piece].astype(F32)
        even_b, odd_b = jnp.where(is_odd, other, mine), jnp.where(is_odd, mine, other)
        even_d = jnp.where(is_odd, rdec[piece], dec[pl.ds(base + c * size, size)])
        odd_d = jnp.where(is_odd, dec[pl.ds(base + c * size, size)], rdec[piece])
        middle = odd_d * x + odd_b
        return jnp.where(is_odd, x, middle), jnp.where(is_odd, middle, x), even_d * middle + even_b

    def hop(c, join, landing, stage, send, recv, to, first, last, out, gift, gsend, grecv):
        piece = pl.ds(c * size, size)

        @pl.when(first)
        def _():
            landing[piece] = jnp.zeros((size,) + landing.shape[1:], landing.dtype)

        @pl.when(jnp.logical_not(first))
        def _():
            copy(stage, landing, send, recv, c, to).wait_recv()

        mine, other, on = join(c, landing[piece].astype(F32))
        stage[piece] = on.astype(BF16)

        @pl.when(jnp.logical_not(last))
        def _():
            copy(stage, landing, send, recv, c, to).start()

        out[pl.ds(base + c * size, size)] = mine.astype(BF16)
        gift[piece] = other.astype(BF16)
        give(gift, out, gsend, grecv, c, base).start()

    def lend(kv, off, to):
        return pltpu.make_async_remote_copy(
            src_ref=part.at[kv, to], dst_ref=land.at[kv, off], send_sem=ps.at[kv, off],
            recv_sem=pr.at[kv, off], **peer(seq=to))

    scale = D ** (-0.5)
    upos = lax.broadcasted_iota(jnp.int32, (length, rows), 0)
    tpos = lax.broadcasted_iota(jnp.int32, (length, rows), 1)

    def attend(h):
        kv = h // ratio
        lanes = pl.ds(pl.multiple_of(h * D, D), D)
        k = kva[:, :, pl.ds(pl.multiple_of(kv * D, D), D)].reshape(length, D)
        v = kva[:, :, pl.ds(pl.multiple_of((kv_heads + kv) * D, D), D)].reshape(length, D)

        @pl.when(lax.rem(h, ratio) == 0)
        def _():
            kt[...] = jnp.transpose(k.astype(F32)).astype(BF16)
            vt[...] = jnp.transpose(v.astype(F32)).astype(BF16)
            dka[...] = jnp.zeros_like(dka)
            dva[...] = jnp.zeros_like(dva)

        q = q_ref[:, lanes]
        dm = dm_ref[:, lanes]
        s = mm_nt(k, q)
        s = jnp.where(upos <= tpos + me * rows, s * (scale * math.log2(math.e)), -1e30)
        e = jnp.exp2(s - jnp.max(s, axis=0, keepdims=True))
        p = e * (1.0 / jnp.sum(e, axis=0, keepdims=True))
        pb = p.astype(BF16)
        att_t = mm(vt[...], pb)
        att_ref[:, lanes] = jnp.transpose(att_t)
        delta = jnp.sum(jnp.transpose(dm.astype(F32)) * att_t, axis=0, keepdims=True)
        ds = (p * (mm_nt(v, dm) - delta)).astype(BF16)
        dq_ref[:, lanes] = jnp.transpose(mm(kt[...], ds)) * scale
        dka[...] += mm(ds, q)
        dva[...] += mm(pb, dm)

        @pl.when(lax.rem(h, ratio) == ratio - 1)
        def _():
            part[kv, :, :, :D] = (dka[...] * scale).astype(BF16).reshape(n, rows, D)
            part[kv, :, :, D:] = dva[...].astype(BF16).reshape(n, rows, D)
            for off in range(1, n):
                @pl.when(me - off >= 0)
                def _():
                    lend(kv, off, lax.rem(me - off + n, n)).start()

    def step(t, carry):
        f = t - level
        b = t - (levels - 1 - level)

        @pl.when(jnp.logical_and(f >= 0, f < chunks))
        def _():
            hop(f, ahead, af, sf, fs, fr, up, level == 0, level == levels - 1,
                s_in, mf, mfs, mfr)

        @pl.when(jnp.logical_and(b >= 0, b < chunks))
        def _():
            hop(b, behind, ab, sb, bs, br, down, level == levels - 1, level == 0,
                g_in, mb, mbs, mbr)

        @pl.when(t < heads)
        def _():
            attend(t)

        return carry

    lax.fori_loop(0, max(levels - 1 + chunks, heads), step, 0)

    def drain(c, carry):
        @pl.when(level < levels - 1)
        def _():
            copy(sf, af, fs, fr, c, up).wait_send()

        @pl.when(level > 0)
        def _():
            copy(sb, ab, bs, br, c, down).wait_send()

        give(mf, s_in, mfs, mfr, c, base).wait_send()
        give(mb, g_in, mbs, mbr, c, base).wait_send()
        give(mf, s_in, mfs, mfr, c, share - base).wait_recv()
        give(mb, g_in, mbs, mbr, c, share - base).wait_recv()

        return carry

    lax.fori_loop(0, chunks, drain, 0)
    b = bcv_ref[:, :D]
    c = bcv_ref[:, D:]
    inner[...] = mm_nt(c, b)
    dinner[...] = jnp.zeros_like(dinner)
    dbc[...] = jnp.zeros_like(dbc)

    def ssd(h, carry):
        lanes = pl.ds(pl.multiple_of(h * D, D), D)
        dm = dm_ref[:, lanes]
        dmf = dm.astype(F32)
        w = w_ref[:, lanes].astype(F32)
        pre = conv(x_ref[:, lanes].astype(F32), xh_ref[:, lanes].astype(F32), w)
        sig = sigmoid(pre)
        xb = (pre * sig).astype(BF16)
        xf = xb.astype(F32)
        row = run_ref[h]
        col = columns(row)
        final = row[:, rows - 1:]
        t_i = lax.broadcasted_iota(jnp.int32, (rows, rows), 0)
        s_i = lax.broadcasted_iota(jnp.int32, (rows, rows), 1)
        fade = jnp.exp(jnp.where(t_i >= s_i, col - row, -1e30))
        mix = inner[...] * fade
        skip = skip_ref[h]
        enter = jnp.exp(col)
        tail = jnp.exp(final - col)
        state = s_in[h]
        grad = g_in[h]
        carried = enter * mm(c, state)
        y = mm(mix.astype(BF16), xb) + carried + skip * xf
        mixed_ref[:, lanes] = (y + att_ref[:, lanes]).astype(BF16)
        back = tail * mm(b, grad)
        gx = mm(jnp.transpose(mix).astype(BF16), dm) + back + skip * dmf
        dmix = mm_nt(dm, xb)
        dinner[...] += dmix * fade
        dbc[:, D:] += mm_nt((enter * dmf).astype(BF16), state)
        dbc[:, :D] += mm_nt((tail * xf).astype(BF16), grad)
        dgap = dmix * mix
        away = xf * back
        net = dgap - jnp.transpose(dgap) + dmf * carried - away
        net = jnp.sum(net, axis=1, keepdims=True)
        dfinal = jnp.sum(away) + jnp.sum(
            jnp.exp(final) * jnp.sum(state.astype(F32) * grad.astype(F32), axis=0, keepdims=True))
        dla_ref[h] = jnp.sum(jnp.where(t_i >= s_i, net, 0.0), axis=0, keepdims=True) + dfinal

        g = gx * (sig * (1.0 + pre * (1.0 - sig)))
        gh_ref[:, lanes] = g[:EDGE].astype(BF16)
        width = w.shape[0]
        padded = jnp.concatenate([g, jnp.zeros((8, D), F32)], axis=0)
        total = None
        for tap in range(width):
            offset = width - 1 - tap
            term = w[tap:tap + 1] * padded[offset:offset + rows]
            total = term if total is None else total + term
        dx_ref[:, lanes] = total
        return carry

    lax.fori_loop(0, heads, ssd, 0)
    di = dinner[...]
    dbc_ref[:, D:] = (dbc[:, D:] + mm(di.astype(BF16), b)).astype(BF16)
    dbc_ref[:, :D] = (dbc[:, :D] + mm(jnp.transpose(di).astype(BF16), c)).astype(BF16)

    for kv in range(kv_heads):
        cols = slice(kv * D, kv * D + D)
        own = part[kv, me].astype(F32)
        dk_out[:, cols] = own[:, :D]
        dv_out[:, cols] = own[:, D:]
        for off in range(1, n):
            @pl.when(me + off < n)
            def _():
                lend(kv, off, prv).wait_recv()
                came = land[kv, off].astype(F32)
                dk_out[:, cols] += came[:, :D]
                dv_out[:, cols] += came[:, D:]

    for kv in range(kv_heads):
        for off in range(1, n):
            @pl.when(me - off >= 0)
            def _():
                lend(kv, off, lax.rem(me - off + n, n)).wait_send()


def chain(n, of, ob, rf, rb, dec, rdec, kva, queries, d_mixed, x_in, xh, conv_x, bcv, run_rows,
          skip_rows):
    share = of.shape[0]
    rows, wide = queries.shape
    width = kva.shape[2] // 2
    kv_heads = width // D
    size = 2 if share % 2 == 0 else 1
    chunks = share // size
    dma = pltpu.SemaphoreType.DMA
    shape = jax.ShapeDtypeStruct
    states = pltpu.VMEM((2 * share, D, D), BF16)
    return pl.pallas_call(
        functools.partial(chain_kernel, n, size),
        out_shape=(shape((rows, wide), F32), shape((rows, width), F32), shape((rows, width), F32),
                   shape((rows, wide), BF16), shape((rows, wide), F32), shape((EDGE, wide), BF16),
                   shape((2 * share, 1, rows), F32), shape(bcv.shape, BF16)),
        in_specs=[VMEM] * 15,
        out_specs=(VMEM,) * 8,
        scratch_shapes=[
            states, states, pltpu.VMEM((rows, wide), F32), pltpu.VMEM((rows, rows), F32),
            pltpu.VMEM((rows, rows), F32), pltpu.VMEM(bcv.shape, F32),
            *[pltpu.VMEM(of.shape, BF16) for _ in range(6)],
            pltpu.VMEM((D, n * rows), BF16), pltpu.VMEM((D, n * rows), BF16),
            pltpu.VMEM((n * rows, D), F32), pltpu.VMEM((n * rows, D), F32),
            pltpu.VMEM((kv_heads, n, rows, 2 * D), BF16), pltpu.VMEM((kv_heads, n, rows, 2 * D), BF16),
            *[dma((chunks,)) for _ in range(8)],
            dma((kv_heads, n)), dma((kv_heads, n))],
        compiler_params=pltpu.CompilerParams(
            collective_id=1, has_side_effects=True, vmem_limit_bytes=28 * 2**20),
        name="chain",
    )(of, ob, rf, rb, dec, rdec, kva, queries, d_mixed, x_in, xh, conv_x, bcv, run_rows, skip_rows)


def sums_kernel(n, m, bc_ref, gh_ref, bc_out, bcn_out, gn_out, bb, nb, bs, br, ns, nr, hs, hr):
    me = lax.axis_index("seq")
    my = lax.axis_index("head")
    nxt = lax.rem(me + 1, n)
    prv = lax.rem(me + n - 1, n)
    barrier = pltpu.get_barrier_semaphore()
    count = 0
    for to in (nxt, prv):
        pl.semaphore_signal(barrier, inc=1, **peer(seq=to, head=my))
        count += 1
    for off in range(1, m):
        other = lax.rem(my + off, m)
        for to in (me, nxt, prv):
            pl.semaphore_signal(barrier, inc=1, **peer(seq=to, head=other))
            count += 1
    pl.semaphore_wait(barrier, count)

    def remote(src, dst, send, recv, seq, head):
        return pltpu.make_async_remote_copy(
            src_ref=src, dst_ref=dst, send_sem=send, recv_sem=recv, **peer(seq=seq, head=head))

    def across(off):
        return remote(bc_ref, bb.at[off], bs.at[off], br.at[off], me, lax.rem(my + off, m))

    def before(off):
        return remote(bc_ref.at[pl.ds(0, EDGE)], nb.at[off], ns.at[off], nr.at[off], prv,
                      lax.rem(my + off, m))

    edge = remote(gh_ref, gn_out, hs, hr, prv, my)
    for off in range(1, m):
        across(off).start()

    @pl.when(me > 0)
    def _():
        edge.start()
        for off in range(m):
            before(off).start()

    total = bc_ref[...].astype(F32)
    for off in range(1, m):
        across(off).wait_recv()
        total += bb[off].astype(F32)
    bc_out[...] = total

    @pl.when(me < n - 1)
    def _():
        edge.wait_recv()
        after = None
        for off in range(m):
            before(off).wait_recv()
            part = nb[off].astype(F32)
            after = part if after is None else after + part
        bcn_out[...] = after

    @pl.when(me == n - 1)
    def _():
        gn_out[...] = jnp.zeros(gn_out.shape, gn_out.dtype)
        bcn_out[...] = jnp.zeros(bcn_out.shape, bcn_out.dtype)

    for off in range(1, m):
        across(off).wait_send()

    @pl.when(me > 0)
    def _():
        edge.wait_send()
        for off in range(m):
            before(off).wait_send()


def sums(n, m, dbc, gh):
    dma = pltpu.SemaphoreType.DMA
    shape = jax.ShapeDtypeStruct
    return pl.pallas_call(
        functools.partial(sums_kernel, n, m),
        out_shape=(shape(dbc.shape, F32), shape((EDGE, dbc.shape[1]), F32), shape(gh.shape, BF16)),
        in_specs=[VMEM] * 2,
        out_specs=(VMEM,) * 3,
        scratch_shapes=[
            pltpu.VMEM((m,) + dbc.shape, BF16), pltpu.VMEM((m, EDGE, dbc.shape[1]), BF16),
            dma((m,)), dma((m,)), dma((m,)), dma((m,)), dma, dma],
        compiler_params=pltpu.CompilerParams(collective_id=2, has_side_effects=True),
        name="sums",
    )(dbc, gh)


def silu_slope(pre):
    s = jax.nn.sigmoid(pre)
    return s * (1.0 + pre * (1.0 - s))


def shards(n, m, x_in, bc_in, conv_x, conv_bc, log_decay, skip, queries, keys, values, d_mixed):
    rows = x_in.shape[0]
    heads = x_in.shape[1] // D
    taps = conv_x.shape[0]
    edge = taps - 1
    bc = bc_in.reshape(rows, 2 * D)
    wbc = conv_bc.reshape(taps, 2 * D)
    running = jnp.cumsum(log_decay, axis=0)
    run_rows = running.T.reshape(heads, 1, rows)
    dec = jnp.broadcast_to(jnp.exp(running[-1])[:, None, None], (heads, 1, D))
    skip_rows = jnp.broadcast_to(skip[:, None, None], (heads, 1, D))
    xh, bch, bcn, kva, bcv, of, ob, rf, rb, rdec = first_part(
        n, x_in, bc, keys, values, conv_x, wbc, run_rows, d_mixed, dec)
    dq, d_keys, d_values, mixed, dx, gh, dla, dbc = chain(
        n, of, ob, rf, rb, dec, rdec, kva, queries, d_mixed, x_in, xh, conv_x, bcv, run_rows,
        skip_rows)
    bcs, bca, gn = sums(n, m, dbc, gh)
    wx = conv_x.astype(F32)
    gnf = jnp.concatenate([jnp.zeros((edge, gn.shape[1]), F32), gn[:edge].astype(F32)], axis=0)
    fix = sum(wx[j] * gnf[edge - j:2 * edge - j] for j in range(taps))
    d_x_in = dx.at[rows - edge:].add(fix)
    wb = wbc.astype(F32)
    full = jnp.concatenate([bch[EDGE - edge:], bc, bcn[:edge]], axis=0).astype(F32)
    pre = sum(wb[j] * full[j:j + rows + edge] for j in range(taps))
    g = jnp.concatenate([bcs, bca[:edge]], axis=0) * silu_slope(pre)
    d_bc = sum(wb[j] * g[edge - j:edge - j + rows] for j in range(taps))
    return (mixed, dq, d_keys, d_values, d_x_in, d_bc.reshape(rows, 2, D), dla.reshape(heads, rows).T)


def solution(mesh):
    n, m = mesh.shape["seq"], mesh.shape["head"]
    grid = P("seq", "head")
    part = P("seq", None, None)
    in_specs = (grid, part, P(None, "head"), P(), grid, P("head"), grid, grid, grid, grid)
    out_specs = (grid, grid, grid, grid, grid, part, grid)
    return jax.shard_map(functools.partial(shards, n, m), mesh=mesh, in_specs=in_specs,
                         out_specs=out_specs, check_vma=False)
```

```python
import functools
import math

import jax
import jax.numpy as jnp
from jax import lax
from jax.experimental import pallas as pl
from jax.experimental.pallas import tpu as pltpu
from jax.sharding import PartitionSpec as P

D = 128
EDGE = 16
F32 = jnp.float32
BF16 = jnp.bfloat16
MESH = pl.DeviceIdType.MESH
VMEM = pl.BlockSpec(memory_space=pltpu.VMEM)
ANY = pl.BlockSpec(memory_space=pl.ANY)


def mm(a, b):
    return jnp.dot(a, b, preferred_element_type=F32)


def mm_nt(a, b):
    return lax.dot_general(a, b, (((1,), (1,)), ((), ())), preferred_element_type=F32)


def sigmoid(v):
    return 1.0 / (1.0 + jnp.exp(-v))


def peer(**coords):
    return dict(device_id=coords, device_id_type=MESH)


def conv(x, halo, taps):
    width = taps.shape[0]
    rows = x.shape[0]
    full = jnp.concatenate([halo[EDGE - 8:], x], axis=0)
    total = None
    for tap in range(width):
        start = 8 - (width - 1) + tap
        term = taps[tap:tap + 1] * full[start:start + rows]
        total = term if total is None else total + term
    return total


def columns(row):
    return jnp.transpose(jnp.broadcast_to(row, (D, row.shape[1])))


def first_kernel(n, x_ref, bc_ref, k_ref, v_ref, w_ref, wbc_ref, run_ref, dm_ref, dec_ref,
                 xh, bch, bcn, kva, bcv_ref, of_ref, ob_ref, rf_ref, rb_ref, rdec_ref,
                 sf, sb, bt, ct, zs, zr, fs, fr, hs, hr, ofs, ofr, obs, obr, es, er):
    me = lax.axis_index("seq")
    odd = lax.rem(me, 2)
    mate = me + 1 - 2 * odd
    half = n // 2
    rows = x_ref.shape[0]
    width = k_ref.shape[1]
    heads = x_ref.shape[1] // D
    nxt = lax.rem(me + 1, n)
    prv = lax.rem(me + n - 1, n)
    barrier = pltpu.get_barrier_semaphore()
    for off in range(1, n):
        pl.semaphore_signal(barrier, inc=1, **peer(seq=lax.rem(me + off, n)))
    kva[me, :, :width] = k_ref[...]
    kva[me, :, width:] = v_ref[...]
    pl.semaphore_wait(barrier, n - 1)

    def halo(slot, src, dst, to):
        return pltpu.make_async_remote_copy(
            src_ref=src, dst_ref=dst, send_sem=hs.at[slot], recv_sem=hr.at[slot], **peer(seq=to))

    last = pl.ds(rows - EDGE, EDGE)
    cx = halo(0, x_ref.at[last], xh, nxt)
    cb = halo(1, bc_ref.at[last], bch, nxt)
    cn = halo(2, bc_ref.at[pl.ds(0, EDGE)], bcn, prv)

    @pl.when(me < n - 1)
    def _():
        cb.start()
        cx.start()

    @pl.when(me > 0)
    def _():
        cn.start()

    share = heads // 2
    swap = pltpu.make_async_remote_copy(
        src_ref=dec_ref.at[pl.ds((1 - odd) * share, share)], dst_ref=rdec_ref, send_sem=es,
        recv_sem=er, **peer(seq=mate))
    swap.start()

    def trade(i):
        return (
            pltpu.make_async_remote_copy(
                src_ref=sf.at[i], dst_ref=rf_ref.at[i], send_sem=ofs.at[i], recv_sem=ofr.at[i],
                **peer(seq=mate)),
            pltpu.make_async_remote_copy(
                src_ref=sb.at[i], dst_ref=rb_ref.at[i], send_sem=obs.at[i], recv_sem=obr.at[i],
                **peer(seq=mate)),
        )

    def block(src, to, send, recv):
        return pltpu.make_async_remote_copy(
            src_ref=kva.at[src], dst_ref=kva.at[src], send_sem=send, recv_sem=recv, **peer(seq=to))

    def direct(k):
        return block(me, lax.rem(me + 2 * k, n), zs.at[k], zr.at[k])

    def arrive(k):
        return block(lax.rem(me - 2 * k + n, n), lax.rem(me + 2 * k, n), zs.at[k], zr.at[k])

    def forward(k):
        return block(lax.rem(me - 2 * k + n, n), mate, fs.at[k], fr.at[k])

    def handed(k):
        return block(lax.rem(mate - 2 * k + n, n), mate, fs.at[k], fr.at[k])

    for k in range(1, half):
        @pl.when(me + 2 * k < n)
        def _():
            direct(k).start()

    @pl.when(odd == 0)
    def _():
        forward(0).start()

    for off in range(1, n):
        @pl.when(me + off < n)
        def _():
            kva[lax.rem(me + off, n)] = jnp.zeros(kva.shape[1:], kva.dtype)

    @pl.when(me == 0)
    def _():
        xh[...] = jnp.zeros(xh.shape, xh.dtype)
        bch[...] = jnp.zeros(bch.shape, bch.dtype)

    @pl.when(me == n - 1)
    def _():
        bcn[...] = jnp.zeros(bcn.shape, bcn.dtype)

    @pl.when(me > 0)
    def _():
        cb.wait_recv()
        cx.wait_recv()

    pre = conv(bc_ref[...].astype(F32), bch[...].astype(F32), wbc_ref[...].astype(F32))
    act = (pre * sigmoid(pre)).astype(BF16)
    bcv_ref[...] = act
    act = act.astype(F32)
    bt[...] = jnp.transpose(act[:, :D]).astype(BF16)
    ct[...] = jnp.transpose(act[:, D:]).astype(BF16)

    def head(i, carry):
        h = lax.rem(i + (1 - odd) * share, heads)
        lanes = pl.ds(pl.multiple_of(h * D, D), D)
        pre = conv(x_ref[:, lanes].astype(F32), xh[:, lanes].astype(F32), w_ref[:, lanes].astype(F32))
        xc = (pre * sigmoid(pre)).astype(BF16).astype(F32)
        row = run_ref[h]
        col = columns(row)
        final = row[:, rows - 1:]
        own_f = mm(bt[...], (xc * jnp.exp(final - col)).astype(BF16))
        own_b = mm(ct[...], (dm_ref[:, lanes].astype(F32) * jnp.exp(col)).astype(BF16))

        @pl.when(i < share)
        def _():
            sf[i] = own_f.astype(BF16)
            sb[i] = own_b.astype(BF16)
            for cp in trade(i):
                cp.start()

        @pl.when(i >= share)
        def _():
            of_ref[i - share] = own_f
            ob_ref[i - share] = own_b

        return carry

    done = 0
    for k in range(1, half):
        upto = heads * k // half
        lax.fori_loop(done, upto, head, 0)
        done = upto

        @pl.when(me - 2 * k >= 0)
        def _():
            arrive(k).wait_recv()
            forward(k).start()

    lax.fori_loop(done, heads, head, 0)
    swap.wait()

    def settle(i, carry):
        for cp in trade(i):
            cp.wait()
        return carry

    lax.fori_loop(0, share, settle, 0)

    @pl.when(me < n - 1)
    def _():
        cb.wait_send()
        cx.wait_send()
        cn.wait_recv()

    @pl.when(me > 0)
    def _():
        cn.wait_send()

    @pl.when(odd == 0)
    def _():
        forward(0).wait_send()

    @pl.when(odd == 1)
    def _():
        handed(0).wait_recv()

    for k in range(1, half):
        @pl.when(me + 2 * k < n)
        def _():
            direct(k).wait_send()

        @pl.when(me - 2 * k >= 0)
        def _():
            forward(k).wait_send()

        @pl.when(mate - 2 * k >= 0)
        def _():
            handed(k).wait_recv()


def first_part(n, x_in, bc, keys, values, conv_x, conv_bc, run_rows, d_mixed, dec):
    rows, width = keys.shape
    share = x_in.shape[1] // D // 2
    dma = pltpu.SemaphoreType.DMA
    shape = jax.ShapeDtypeStruct
    return pl.pallas_call(
        functools.partial(first_kernel, n),
        out_shape=(
            shape((EDGE, x_in.shape[1]), BF16), shape((EDGE, bc.shape[1]), BF16),
            shape((EDGE, bc.shape[1]), BF16), shape((n, rows, 2 * width), BF16),
            shape(bc.shape, BF16), shape((share, D, D), F32), shape((share, D, D), F32),
            shape((share, D, D), BF16), shape((share, D, D), BF16), shape((share, 1, D), F32),
        ),
        in_specs=[VMEM] * 9,
        out_specs=(VMEM,) * 10,
        scratch_shapes=[pltpu.VMEM((share, D, D), BF16), pltpu.VMEM((share, D, D), BF16),
                        pltpu.VMEM((D, rows), BF16), pltpu.VMEM((D, rows), BF16),
                        dma((n // 2,)), dma((n // 2,)), dma((n // 2,)), dma((n // 2,)),
                        dma((3,)), dma((3,)), dma((share,)), dma((share,)), dma((share,)),
                        dma((share,)), dma, dma],
        compiler_params=pltpu.CompilerParams(
            collective_id=0, has_side_effects=True, vmem_limit_bytes=20 * 2**20),
        name="first",
    )(x_in, bc, keys, values, conv_x, conv_bc, run_rows, d_mixed, dec)


def chain_kernel(n, size, of, ob, rf, rb, dec, rdec, kva, q_ref, dm_ref,
                 x_ref, xh_ref, w_ref, bcv_ref, run_ref, skip_ref,
                 dq_ref, dk_out, dv_out, mixed_ref, dx_ref, gh_ref, dla_ref, dbc_ref,
                 s_in, g_in, att_ref, inner, dinner, dbc, af, ab, sf, sb, mf, mb, kt, vt, dka, dva, part, land,
                 fs, fr, bs, br, mfs, mfr, mbs, mbr, ps, pr):
    me = lax.axis_index("seq")
    share = of.shape[0]
    chunks = share // size
    rows, wide = q_ref.shape
    heads = wide // D
    kv_heads = kva.shape[2] // (2 * D)
    ratio = heads // kv_heads
    length = n * rows
    odd = lax.rem(me, 2)
    mate = me + 1 - 2 * odd
    base = odd * share
    level = me // 2
    levels = n // 2
    up = lax.rem(me + 2, n)
    down = lax.rem(me + n - 2, n)
    prv = lax.rem(me + n - 1, n)
    barrier = pltpu.get_barrier_semaphore()
    for off in range(1, n):
        pl.semaphore_signal(barrier, inc=1, **peer(seq=lax.rem(me + off, n)))
    pl.semaphore_wait(barrier, n - 1)

    def copy(stage, landing, send, recv, c, to):
        piece = pl.ds(c * size, size)
        return pltpu.make_async_remote_copy(
            src_ref=stage.at[piece], dst_ref=landing.at[piece], send_sem=send.at[c],
            recv_sem=recv.at[c], **peer(seq=to))

    def give(stage, out, send, recv, c, start):
        return pltpu.make_async_remote_copy(
            src_ref=stage.at[pl.ds(c * size, size)], dst_ref=out.at[pl.ds(start + c * size, size)],
            send_sem=send.at[c], recv_sem=recv.at[c], **peer(seq=mate))

    is_odd = odd == 1

    def ahead(c, x):
        piece = pl.ds(c * size, size)
        mine, other = of[piece], rf[piece].astype(F32)
        even_f, odd_f = jnp.where(is_odd, other, mine), jnp.where(is_odd, mine, other)
        even_d = jnp.where(is_odd, rdec[piece], dec[pl.ds(base + c * size, size)])
        odd_d = jnp.where(is_odd, dec[pl.ds(base + c * size, size)], rdec[piece])
        middle = even_d * x + even_f
        return jnp.where(is_odd, middle, x), jnp.where(is_odd, x, middle), odd_d * middle + odd_f

    def behind(c, x):
        piece = pl.ds(c * size, size)
        mine, other = ob[piece], rb[piece].astype(F32)
        even_b, odd_b = jnp.where(is_odd, other, mine), jnp.where(is_odd, mine, other)
        even_d = jnp.where(is_odd, rdec[piece], dec[pl.ds(base + c * size, size)])
        odd_d = jnp.where(is_odd, dec[pl.ds(base + c * size, size)], rdec[piece])
        middle = odd_d * x + odd_b
        return jnp.where(is_odd, x, middle), jnp.where(is_odd, middle, x), even_d * middle + even_b

    def hop(c, join, landing, stage, send, recv, to, first, last, out, gift, gsend, grecv):
        piece = pl.ds(c * size, size)

        @pl.when(first)
        def _():
            landing[piece] = jnp.zeros((size,) + landing.shape[1:], landing.dtype)

        @pl.when(jnp.logical_not(first))
        def _():
            copy(stage, landing, send, recv, c, to).wait_recv()

        mine, other, on = join(c, landing[piece].astype(F32))
        stage[piece] = on.astype(BF16)

        @pl.when(jnp.logical_not(last))
        def _():
            copy(stage, landing, send, recv, c, to).start()

        out[pl.ds(base + c * size, size)] = mine.astype(BF16)
        gift[piece] = other.astype(BF16)
        give(gift, out, gsend, grecv, c, base).start()

    def lend(kv, off, to):
        return pltpu.make_async_remote_copy(
            src_ref=part.at[kv, to], dst_ref=land.at[kv, off], send_sem=ps.at[kv, off],
            recv_sem=pr.at[kv, off], **peer(seq=to))

    scale = D ** (-0.5)
    upos = lax.broadcasted_iota(jnp.int32, (length, rows), 0)
    tpos = lax.broadcasted_iota(jnp.int32, (length, rows), 1)

    def attend(h):
        kv = h // ratio
        lanes = pl.ds(pl.multiple_of(h * D, D), D)
        k = kva[:, :, pl.ds(pl.multiple_of(kv * D, D), D)].reshape(length, D)
        v = kva[:, :, pl.ds(pl.multiple_of((kv_heads + kv) * D, D), D)].reshape(length, D)

        @pl.when(lax.rem(h, ratio) == 0)
        def _():
            kt[...] = jnp.transpose(k.astype(F32)).astype(BF16)
            vt[...] = jnp.transpose(v.astype(F32)).astype(BF16)
            dka[...] = jnp.zeros_like(dka)
            dva[...] = jnp.zeros_like(dva)

        q = q_ref[:, lanes]
        dm = dm_ref[:, lanes]
        s = mm_nt(k, q)
        s = jnp.where(upos <= tpos + me * rows, s * (scale * math.log2(math.e)), -1e30)
        e = jnp.exp2(s - jnp.max(s, axis=0, keepdims=True))
        p = e * (1.0 / jnp.sum(e, axis=0, keepdims=True))
        pb = p.astype(BF16)
        att_t = mm(vt[...], pb)
        att_ref[:, lanes] = jnp.transpose(att_t)
        delta = jnp.sum(jnp.transpose(dm.astype(F32)) * att_t, axis=0, keepdims=True)
        ds = (p * (mm_nt(v, dm) - delta)).astype(BF16)
        dq_ref[:, lanes] = jnp.transpose(mm(kt[...], ds)) * scale
        dka[...] += mm(ds, q)
        dva[...] += mm(pb, dm)

        @pl.when(lax.rem(h, ratio) == ratio - 1)
        def _():
            part[kv, :, :, :D] = (dka[...] * scale).astype(BF16).reshape(n, rows, D)
            part[kv, :, :, D:] = dva[...].astype(BF16).reshape(n, rows, D)
            for off in reversed(range(1, n)):
                @pl.when(me - off >= 0)
                def _():
                    lend(kv, off, lax.rem(me - off + n, n)).start()

    def step(t, carry):
        f = t - level
        b = t - (levels - 1 - level)

        @pl.when(jnp.logical_and(f >= 0, f < chunks))
        def _():
            hop(f, ahead, af, sf, fs, fr, up, level == 0, level == levels - 1,
                s_in, mf, mfs, mfr)

        @pl.when(jnp.logical_and(b >= 0, b < chunks))
        def _():
            hop(b, behind, ab, sb, bs, br, down, level == levels - 1, level == 0,
                g_in, mb, mbs, mbr)

        @pl.when(t < heads)
        def _():
            attend(t)

        return carry

    lax.fori_loop(0, max(levels - 1 + chunks, heads), step, 0)

    def drain(c, carry):
        @pl.when(level < levels - 1)
        def _():
            copy(sf, af, fs, fr, c, up).wait_send()

        @pl.when(level > 0)
        def _():
            copy(sb, ab, bs, br, c, down).wait_send()

        give(mf, s_in, mfs, mfr, c, base).wait_send()
        give(mb, g_in, mbs, mbr, c, base).wait_send()
        give(mf, s_in, mfs, mfr, c, share - base).wait_recv()
        give(mb, g_in, mbs, mbr, c, share - base).wait_recv()

        return carry

    lax.fori_loop(0, chunks, drain, 0)
    b = bcv_ref[:, :D]
    c = bcv_ref[:, D:]
    inner[...] = mm_nt(c, b)
    dinner[...] = jnp.zeros_like(dinner)
    dbc[...] = jnp.zeros_like(dbc)

    def ssd(h, carry):
        lanes = pl.ds(pl.multiple_of(h * D, D), D)
        dm = dm_ref[:, lanes]
        dmf = dm.astype(F32)
        w = w_ref[:, lanes].astype(F32)
        pre = conv(x_ref[:, lanes].astype(F32), xh_ref[:, lanes].astype(F32), w)
        sig = sigmoid(pre)
        xb = (pre * sig).astype(BF16)
        xf = xb.astype(F32)
        row = run_ref[h]
        col = columns(row)
        final = row[:, rows - 1:]
        t_i = lax.broadcasted_iota(jnp.int32, (rows, rows), 0)
        s_i = lax.broadcasted_iota(jnp.int32, (rows, rows), 1)
        fade = jnp.exp(jnp.where(t_i >= s_i, col - row, -1e30))
        mix = inner[...] * fade
        skip = skip_ref[h]
        enter = jnp.exp(col)
        tail = jnp.exp(final - col)
        state = s_in[h]
        grad = g_in[h]
        carried = enter * mm(c, state)
        y = mm(mix.astype(BF16), xb) + carried + skip * xf
        mixed_ref[:, lanes] = (y + att_ref[:, lanes]).astype(BF16)
        back = tail * mm(b, grad)
        gx = mm(jnp.transpose(mix).astype(BF16), dm) + back + skip * dmf
        dmix = mm_nt(dm, xb)
        dinner[...] += dmix * fade
        dbc[:, D:] += mm_nt((enter * dmf).astype(BF16), state)
        dbc[:, :D] += mm_nt((tail * xf).astype(BF16), grad)
        dgap = dmix * mix
        away = xf * back
        net = dgap - jnp.transpose(dgap) + dmf * carried - away
        net = jnp.sum(net, axis=1, keepdims=True)
        dfinal = jnp.sum(away) + jnp.sum(
            jnp.exp(final) * jnp.sum(state.astype(F32) * grad.astype(F32), axis=0, keepdims=True))
        dla_ref[h] = jnp.sum(jnp.where(t_i >= s_i, net, 0.0), axis=0, keepdims=True) + dfinal

        g = gx * (sig * (1.0 + pre * (1.0 - sig)))
        gh_ref[:, lanes] = g[:EDGE].astype(BF16)
        width = w.shape[0]
        padded = jnp.concatenate([g, jnp.zeros((8, D), F32)], axis=0)
        total = None
        for tap in range(width):
            offset = width - 1 - tap
            term = w[tap:tap + 1] * padded[offset:offset + rows]
            total = term if total is None else total + term
        dx_ref[:, lanes] = total
        return carry

    lax.fori_loop(0, heads, ssd, 0)
    di = dinner[...]
    dbc_ref[:, D:] = (dbc[:, D:] + mm(di.astype(BF16), b)).astype(BF16)
    dbc_ref[:, :D] = (dbc[:, :D] + mm(jnp.transpose(di).astype(BF16), c)).astype(BF16)

    for kv in range(kv_heads):
        cols = slice(kv * D, kv * D + D)
        own = part[kv, me].astype(F32)
        dk_out[:, cols] = own[:, :D]
        dv_out[:, cols] = own[:, D:]
        for off in range(1, n):
            @pl.when(me + off < n)
            def _():
                lend(kv, off, prv).wait_recv()
                came = land[kv, off].astype(F32)
                dk_out[:, cols] += came[:, :D]
                dv_out[:, cols] += came[:, D:]

    for kv in range(kv_heads):
        for off in range(1, n):
            @pl.when(me - off >= 0)
            def _():
                lend(kv, off, lax.rem(me - off + n, n)).wait_send()


def chain(n, of, ob, rf, rb, dec, rdec, kva, queries, d_mixed, x_in, xh, conv_x, bcv, run_rows,
          skip_rows):
    share = of.shape[0]
    rows, wide = queries.shape
    width = kva.shape[2] // 2
    kv_heads = width // D
    size = 2 if share % 2 == 0 else 1
    chunks = share // size
    dma = pltpu.SemaphoreType.DMA
    shape = jax.ShapeDtypeStruct
    states = pltpu.VMEM((2 * share, D, D), BF16)
    return pl.pallas_call(
        functools.partial(chain_kernel, n, size),
        out_shape=(shape((rows, wide), F32), shape((rows, width), F32), shape((rows, width), F32),
                   shape((rows, wide), BF16), shape((rows, wide), F32), shape((EDGE, wide), BF16),
                   shape((2 * share, 1, rows), F32), shape(bcv.shape, BF16)),
        in_specs=[VMEM] * 15,
        out_specs=(VMEM,) * 8,
        scratch_shapes=[
            states, states, pltpu.VMEM((rows, wide), F32), pltpu.VMEM((rows, rows), F32),
            pltpu.VMEM((rows, rows), F32), pltpu.VMEM(bcv.shape, F32),
            *[pltpu.VMEM(of.shape, BF16) for _ in range(6)],
            pltpu.VMEM((D, n * rows), BF16), pltpu.VMEM((D, n * rows), BF16),
            pltpu.VMEM((n * rows, D), F32), pltpu.VMEM((n * rows, D), F32),
            pltpu.VMEM((kv_heads, n, rows, 2 * D), BF16), pltpu.VMEM((kv_heads, n, rows, 2 * D), BF16),
            *[dma((chunks,)) for _ in range(8)],
            dma((kv_heads, n)), dma((kv_heads, n))],
        compiler_params=pltpu.CompilerParams(
            collective_id=1, has_side_effects=True, vmem_limit_bytes=28 * 2**20),
        name="chain",
    )(of, ob, rf, rb, dec, rdec, kva, queries, d_mixed, x_in, xh, conv_x, bcv, run_rows, skip_rows)


def sums_kernel(n, m, bc_ref, gh_ref, bc_out, bcn_out, gn_out, bb, nb, bs, br, ns, nr, hs, hr):
    me = lax.axis_index("seq")
    my = lax.axis_index("head")
    nxt = lax.rem(me + 1, n)
    prv = lax.rem(me + n - 1, n)
    barrier = pltpu.get_barrier_semaphore()
    count = 0
    for to in (nxt, prv):
        pl.semaphore_signal(barrier, inc=1, **peer(seq=to, head=my))
        count += 1
    for off in range(1, m):
        other = lax.rem(my + off, m)
        for to in (me, nxt, prv):
            pl.semaphore_signal(barrier, inc=1, **peer(seq=to, head=other))
            count += 1
    pl.semaphore_wait(barrier, count)

    def remote(src, dst, send, recv, seq, head):
        return pltpu.make_async_remote_copy(
            src_ref=src, dst_ref=dst, send_sem=send, recv_sem=recv, **peer(seq=seq, head=head))

    def across(off):
        return remote(bc_ref, bb.at[off], bs.at[off], br.at[off], me, lax.rem(my + off, m))

    def before(off):
        return remote(bc_ref.at[pl.ds(0, EDGE)], nb.at[off], ns.at[off], nr.at[off], prv,
                      lax.rem(my + off, m))

    edge = remote(gh_ref, gn_out, hs, hr, prv, my)
    for off in range(1, m):
        across(off).start()

    @pl.when(me > 0)
    def _():
        edge.start()
        for off in range(m):
            before(off).start()

    total = bc_ref[...].astype(F32)
    for off in range(1, m):
        across(off).wait_recv()
        total += bb[off].astype(F32)
    bc_out[...] = total

    @pl.when(me < n - 1)
    def _():
        edge.wait_recv()
        after = None
        for off in range(m):
            before(off).wait_recv()
            part = nb[off].astype(F32)
            after = part if after is None else after + part
        bcn_out[...] = after

    @pl.when(me == n - 1)
    def _():
        gn_out[...] = jnp.zeros(gn_out.shape, gn_out.dtype)
        bcn_out[...] = jnp.zeros(bcn_out.shape, bcn_out.dtype)

    for off in range(1, m):
        across(off).wait_send()

    @pl.when(me > 0)
    def _():
        edge.wait_send()
        for off in range(m):
            before(off).wait_send()


def sums(n, m, dbc, gh):
    dma = pltpu.SemaphoreType.DMA
    shape = jax.ShapeDtypeStruct
    return pl.pallas_call(
        functools.partial(sums_kernel, n, m),
        out_shape=(shape(dbc.shape, F32), shape((EDGE, dbc.shape[1]), F32), shape(gh.shape, BF16)),
        in_specs=[VMEM] * 2,
        out_specs=(VMEM,) * 3,
        scratch_shapes=[
            pltpu.VMEM((m,) + dbc.shape, BF16), pltpu.VMEM((m, EDGE, dbc.shape[1]), BF16),
            dma((m,)), dma((m,)), dma((m,)), dma((m,)), dma, dma],
        compiler_params=pltpu.CompilerParams(collective_id=2, has_side_effects=True),
        name="sums",
    )(dbc, gh)


def finish_kernel(dqi, mixedi, dxi, gn, w_ref, dki, dvi, dq, mixed, dx, dk, dv):
    rows = dx.shape[0]
    taps = w_ref.shape[0]
    dq[...] = dqi[...]
    mixed[...] = mixedi[...]
    w = w_ref[...].astype(F32)
    after = gn[...].astype(F32)[:8]
    after = jnp.concatenate([jnp.zeros_like(after), after], axis=0)
    total = None
    for tap in range(taps):
        offset = taps - 1 - tap
        term = w[tap:tap + 1] * after[offset:offset + 8]
        total = term if total is None else total + term
    dx[:rows - 8] = dxi[:rows - 8]
    dx[rows - 8:] = dxi[rows - 8:] + total

    @pl.when(pl.program_id(0) == 0)
    def _():
        dk[...] = dki[...]
        dv[...] = dvi[...]


def finish(dq, mixed, dx, gn, conv_x, dk, dv):
    rows, wide = dx.shape
    lanes = math.gcd(512, wide)
    cols = lambda a: pl.BlockSpec((a.shape[0], lanes), lambda i: (0, i))
    whole = lambda a: pl.BlockSpec(a.shape, lambda i: (0, 0))
    like = lambda a: jax.ShapeDtypeStruct(a.shape, a.dtype)
    return pl.pallas_call(
        finish_kernel,
        grid=(wide // lanes,),
        out_shape=(like(dq), like(mixed), like(dx), like(dk), like(dv)),
        in_specs=[cols(dq), cols(mixed), cols(dx), cols(gn), cols(conv_x), whole(dk), whole(dv)],
        out_specs=(cols(dq), cols(mixed), cols(dx), whole(dk), whole(dv)),
        name="finish",
    )(dq, mixed, dx, gn, conv_x, dk, dv)


def silu_slope(pre):
    s = jax.nn.sigmoid(pre)
    return s * (1.0 + pre * (1.0 - s))


def shards(n, m, x_in, bc_in, conv_x, conv_bc, log_decay, skip, queries, keys, values, d_mixed):
    rows = x_in.shape[0]
    heads = x_in.shape[1] // D
    taps = conv_x.shape[0]
    edge = taps - 1
    bc = bc_in.reshape(rows, 2 * D)
    wbc = conv_bc.reshape(taps, 2 * D)
    running = jnp.cumsum(log_decay, axis=0)
    run_rows = running.T.reshape(heads, 1, rows)
    dec = jnp.broadcast_to(jnp.exp(running[-1])[:, None, None], (heads, 1, D))
    skip_rows = jnp.broadcast_to(skip[:, None, None], (heads, 1, D))
    xh, bch, bcn, kva, bcv, of, ob, rf, rb, rdec = first_part(
        n, x_in, bc, keys, values, conv_x, wbc, run_rows, d_mixed, dec)
    dq, d_keys, d_values, mixed, dx, gh, dla, dbc = chain(
        n, of, ob, rf, rb, dec, rdec, kva, queries, d_mixed, x_in, xh, conv_x, bcv, run_rows,
        skip_rows)
    bcs, bca, gn = sums(n, m, dbc, gh)
    dq, mixed, d_x_in, d_keys, d_values = finish(dq, mixed, dx, gn, conv_x, d_keys, d_values)
    wb = wbc.astype(F32)
    full = jnp.concatenate([bch[EDGE - edge:], bc, bcn[:edge]], axis=0).astype(F32)
    pre = sum(wb[j] * full[j:j + rows + edge] for j in range(taps))
    g = jnp.concatenate([bcs, bca[:edge]], axis=0) * silu_slope(pre)
    d_bc = sum(wb[j] * g[edge - j:edge - j + rows] for j in range(taps))
    return (mixed, dq, d_keys, d_values, d_x_in, d_bc.reshape(rows, 2, D), dla.reshape(heads, rows).T)


def solution(mesh):
    n, m = mesh.shape["seq"], mesh.shape["head"]
    grid = P("seq", "head")
    part = P("seq", None, None)
    in_specs = (grid, part, P(None, "head"), P(), grid, P("head"), grid, grid, grid, grid)
    out_specs = (grid, grid, grid, grid, grid, part, grid)
    return jax.shard_map(functools.partial(shards, n, m), mesh=mesh, in_specs=in_specs,
                         out_specs=out_specs, check_vma=False)
```
